1024 devices in a mesh: span: 8 (over x), pitch: 8 (over y_lo, core), chord: 16 (over z, y_hi).
Axes of the slice: x: 8, y: 8 (y_hi: 2, y_lo: 4; y = y_hi * 4 + y_lo), z: 8, core: 2. Of those that a mesh axis runs over, the one named last changes fastest.
Arguments:
- adjoint_start: float32 [3, 128, 256, 2048], P(None, 'span', 'pitch', 'chord'), may hold values from -6 to 6
- sensitivity_source: float32 [3, 128, 256, 2048], P(None, 'span', 'pitch', 'chord'), may hold values from -6 to 6
- stiffness_class: int32 [128, 256, 2048], P('span', 'pitch', 'chord'), may hold values from 0 to 7
- stiffness_table: float32 [8], replicated, may hold values from 0.25 to 4
- wall_cell: int32 [4194304], P(('span', 'pitch', 'chord')), may hold values from 0 to 65535
- patch_owner: int32 [4194304, 1], P(('span', 'pitch', 'chord')), may hold values from 0 to 2047; in each aligned block of 4096 rows (0 to 4095, 4096 to 8191, ...) at most 4 rows name the same one
- wall_normal: float32 [3, 4194304], P(None, ('span', 'pitch', 'chord')), may hold values from -1 to 1
- mode_shape: float32 [8, 4194304], P(None, ('span', 'pitch', 'chord')), may hold values from -6 to 6
Outputs:
- adjoint: float32 [3, 128, 256, 2048], P(None, 'span', 'pitch', 'chord')
- patch_grad: float32 [8, 131072], P(None, ('span', 'pitch', 'chord'))
The draws below stay inside these ranges and needn't reach their ends.
Inputs may be any that keep to these rules, and one draw needn't show every extreme that they name: `patch_owner`: within the rows of one device, no patch is named by more than 4 rows, a bound that some block reaches.
All inputs are finite; a program needn't handle non-finite values.
Results may differ from the reference program's by a relative error of at most 0.00018.
Values sent between devices are 32-bit elements; how exact they have to be, the bound alone decides.
No kernel may reach another device: no remote copies, remote signals or barrier semaphores. Data moves between devices by JAX's collectives and lax.ppermute only.
A program may use at most 32 MiB of HBM per device.

```python
import math
import jax
import jax.numpy as jnp
import numpy as np

CX = 16
CY = 32
CZ = 128
PATCH_DEV = 128
CAP = 4
MODES = 8
NCLASS = 8
SWEEPS = 3
NX = 128
NY = 256
NZ = 2048
WALL = 4096
WALL_TOTAL = 4194304
PATCHES = 131072
N_PITCH = 8
N_CHORD = 16


def with_ends(values, stream_key, smallest, largest):
    longest = values.shape.index(max(values.shape))
    spots = []
    for shift in (0, 1):
        where = [jax.random.randint(jax.random.fold_in(stream_key, axis), (), 0, length) for axis, length in enumerate(values.shape)]
        where[longest] = (where[longest] + shift) % values.shape[longest]
        spots.append(tuple(where))
    return values.at[spots[0]].set(smallest).at[spots[1]].set(largest)


def steps_of(stream_key, shape, cuts, low, high):
    level, own = 1.0, jax.random.fold_in(stream_key, 6)
    for dim, shards_of in cuts:
        steps = jnp.exp(jax.random.uniform(jax.random.fold_in(own, dim), (shards_of,), jnp.float32, low / len(cuts), high / len(cuts)))
        level = level * jnp.repeat(steps, shape[dim] // shards_of).reshape([-1 if axis == dim else 1 for axis in range(len(shape))])
    return level


def deal_out(key, own, number, rows, number_of, top, bound, slope):
    ranking = jax.random.permutation(key, number_of)
    crowded, usual = shares(number_of, rows * top, bound, slope, True), shares(number_of, rows * top, bound, slope, False)
    places = jnp.arange(number_of)

    def named(sizes, rotation):
        used = int((sizes > 0).sum())
        fixed = max(1, used // 4)
        moved = fixed + (places - fixed + rotation * (used - fixed)) % max(1, number_of - fixed)
        return jnp.zeros((number_of,), jnp.int32).at[ranking[jnp.where(places < fixed, places, moved)]].set(jnp.asarray(sizes, jnp.int32))

    sizes = jnp.where(number % 4 == 0, named(crowded, number // 4), named(usual, number - number // 4 - 1))
    mixed = jax.random.permutation(jax.random.fold_in(own, 3), number_of)
    giver, receiver = mixed[0:number_of // 2 * 2:2], mixed[1:number_of // 2 * 2:2]
    slack = jnp.minimum(sizes[giver] - 1, bound - sizes[receiver]) // 2
    slack = jnp.where((giver == ranking[0]) | (receiver == ranking[0]) | (sizes[receiver] == 0), 0, jnp.maximum(slack, 0))
    moved = jax.random.randint(jax.random.fold_in(own, 4), (number_of // 2,), 0, 1 << 20) % (slack + 1)
    sizes = sizes.at[giver].add(-moved).at[receiver].add(moved)
    items = jnp.searchsorted(jnp.cumsum(sizes), jnp.arange(rows * top), side="right").astype(jnp.int32)
    listing = items.reshape(top, rows).T
    listing = listing[jax.random.permutation(jax.random.fold_in(own, 1), rows)]
    rotation = jax.random.randint(jax.random.fold_in(own, 2), (rows, 1), 0, top)
    return jnp.take_along_axis(listing, (jnp.arange(top)[None, :] + rotation) % top, axis=1)


def shares(count, total, reach, skew, full):
    weights = [(1 << 20) // math.isqrt(rank ** skew) + 1 for rank in range(1, count + 1)]
    largest = reach if full else min(reach, max(-(-total // count), total * weights[0] // sum(weights)))
    least = 1 if total - largest >= count - 1 else 0
    counts, rest = [largest] + [least] * (count - 1), total - largest - least * (count - 1)
    while rest > 0:
        free = [i for i in range(1, count) if counts[i] < largest] or [i for i in range(1, count) if counts[i] < reach]
        pool, budget = sum([weights[i] for i in free]), rest
        for i in free:
            extra = min(reach - counts[i], max(1, budget * weights[i] // pool), rest)
            counts[i] = counts[i] + extra
            rest = rest - extra
    return np.array(counts)


def gaussian(key, shape, spread, limit, cuts=(), kind=jnp.bfloat16):
    entries = spread * jax.random.normal(key, shape, jnp.float32)
    if cuts:
        entries = entries * steps_of(key, shape, cuts, -0.22, 0.18)
    return jnp.clip(entries, -limit, limit).astype(kind)


def setup_inputs(seed: int = 0) -> dict:
    key_list = jax.random.split(jax.random.key(seed), 9)
    adjoint_start = gaussian(key_list[0], (3, NX, NY, NZ), 1.0, 6.0, ((1, 8), (2, 8), (3, 16)), jnp.float32)
    sensitivity_source = gaussian(key_list[1], (3, NX, NY, NZ), 1.0, 6.0, ((1, 8), (2, 8), (3, 16)), jnp.float32)
    stiffness_class = with_ends(jax.random.randint(key_list[2], (NX, NY, NZ), 0, NCLASS), jax.random.fold_in(key_list[2], 1), 0, NCLASS - 1).astype(jnp.int32)
    stiffness_table = jnp.clip(jnp.exp(jax.random.uniform(key_list[3], (NCLASS,), jnp.float32, math.log(0.25), math.log(4.0))), 0.25, 4.0)
    wall_cell = with_ends(jax.random.randint(key_list[4], (WALL_TOTAL,), 0, CX * CY * CZ), jax.random.fold_in(key_list[4], 1), 0, (CX * CY * CZ) - 1).astype(jnp.int32)
    patch_owner_keys = jax.random.split(jax.random.fold_in(key_list[5], 1), WALL_TOTAL // WALL)
    patch_owner_turns = jax.random.permutation(jax.random.fold_in(key_list[5], 3), WALL_TOTAL // WALL)
    patch_owner = jax.vmap(lambda own, number: deal_out(jax.random.fold_in(key_list[5], 2), own, number, WALL, PATCH_DEV * N_CHORD, 1, CAP, 2))(patch_owner_keys, patch_owner_turns).reshape((WALL_TOTAL, 1))
    wall_normal = jnp.clip(jax.random.uniform(key_list[6], (3, WALL_TOTAL), jnp.float32, -1.0, 1.0) * steps_of(key_list[6], (3, WALL_TOTAL), ((1, 1024),), -0.4, 0.0), -1.0, 1.0)
    mode_shape = gaussian(key_list[7], (MODES, WALL_TOTAL), 1.0, 6.0, ((1, 1024),), jnp.float32)
    return {"adjoint_start": adjoint_start, "sensitivity_source": sensitivity_source, "stiffness_class": stiffness_class, "stiffness_table": stiffness_table, "wall_cell": wall_cell, "patch_owner": patch_owner, "wall_normal": wall_normal, "mode_shape": mode_shape}


MASS_SHIFT = 0.5
RELAXATION = 0.8
DIAGONAL_SUM = 10.5
LAME_WEIGHTS = ((3.0, 1.0, 1.0), (1.0, 3.0, 1.0), (1.0, 1.0, 3.0))


def stiffness_from(classes, table):
    result = jnp.zeros(classes.shape, jnp.float32)
    for number in range(table.shape[0]):
        result = result + jnp.where(classes == number, table[number], 0.0)
    return result


def operator_image(padded):
    center = padded[:, 1:-1, 1:-1, 1:-1]
    along_span = 2.0 * center - padded[:, 2:, 1:-1, 1:-1] - padded[:, :-2, 1:-1, 1:-1]
    along_pitch = 2.0 * center - padded[:, 1:-1, 2:, 1:-1] - padded[:, 1:-1, :-2, 1:-1]
    along_chord = 2.0 * center - padded[:, 1:-1, 1:-1, 2:] - padded[:, 1:-1, 1:-1, :-2]
    weights = jnp.array(LAME_WEIGHTS, jnp.float32)
    image = MASS_SHIFT * center
    image = image + weights[:, 0][:, None, None, None] * along_span
    image = image + weights[:, 1][:, None, None, None] * along_pitch
    image = image + weights[:, 2][:, None, None, None] * along_chord
    return image


def relax_step(adjoint, source, stiffness, image):
    return adjoint + RELAXATION * (source - image) / (DIAGONAL_SUM * stiffness)


def reference(adjoint_start, sensitivity_source, stiffness_class, stiffness_table, wall_cell, patch_owner, wall_normal, mode_shape):
    stiffness = stiffness_from(stiffness_class, stiffness_table)
    adjoint = adjoint_start
    for sweep_index in range(SWEEPS):
        product = stiffness[None] * adjoint
        padded = jnp.pad(product, ((0, 0), (1, 1), (1, 1), (1, 1)))
        adjoint = relax_step(adjoint, sensitivity_source, stiffness, operator_image(padded))
    row_index = jnp.arange(WALL_TOTAL, dtype=jnp.int32)
    device = row_index // WALL
    span_pos = device // (N_PITCH * N_CHORD)
    pitch_pos = (device // N_CHORD) % N_PITCH
    chord_pos = device % N_CHORD
    first_coord = span_pos * CX + wall_cell // (CY * CZ)
    second_coord = pitch_pos * CY + (wall_cell // CZ) % CY
    third_coord = chord_pos * CZ + wall_cell % CZ
    traction_field = stiffness[None] * adjoint
    traction = traction_field[:, first_coord, second_coord, third_coord]
    normal_part = jnp.sum(wall_normal * traction, axis=0)
    contribution = mode_shape * normal_part[None]
    patch_index = ((span_pos * N_PITCH + pitch_pos) * N_CHORD) * PATCH_DEV + patch_owner[:, 0]
    patch_grad = jnp.zeros((MODES, PATCHES), jnp.float32).at[:, patch_index].add(contribution)
    return adjoint, patch_grad
```

```python
import functools

import jax
import jax.numpy as jnp
from jax import lax
from jax.experimental import pallas as pl
from jax.experimental.pallas import tpu as pltpu
from jax.sharding import PartitionSpec as P

CX, CY, CZ = 16, 32, 128
PATCH_DEV = 128
MODES = 8
CHORD = 16
WALL = 4096

MASS_SHIFT = 0.5
RELAXATION = 0.8
DIAGONAL_SUM = 10.5
LAME_WEIGHTS = ((3.0, 1.0, 1.0), (1.0, 3.0, 1.0), (1.0, 1.0, 3.0))

STEP = RELAXATION / DIAGONAL_SUM
OWN = 1.0 - STEP * (MASS_SHIFT + 2.0 * sum(LAME_WEIGHTS[0]))
PULL = tuple(tuple(STEP * weight for weight in row) for row in LAME_WEIGHTS)

GX, GY = 24, 48
LANES = 120
ROWS = 512

VMEM = pl.BlockSpec(memory_space=pltpu.VMEM)
SMEM = pl.BlockSpec(memory_space=pltpu.SMEM)


def iota(shape, dim):
    return lax.broadcasted_iota(jnp.int32, shape, dim)


def shifted_lanes(v):
    lane = iota(v.shape, v.ndim - 1)
    before = jnp.where(lane == 0, 0.0, pltpu.roll(v, 1, v.ndim - 1))
    after = jnp.where(lane == CZ - 1, 0.0, pltpu.roll(v, CZ - 1, v.ndim - 1))
    return before + after


def pick(table, classes):
    low, mid, high = (classes & 1) == 1, (classes & 2) == 2, (classes & 4) == 4
    pairs = [jnp.where(low, table[2 * i + 1], table[2 * i]) for i in range(4)]
    return jnp.where(high, jnp.where(mid, pairs[3], pairs[2]), jnp.where(mid, pairs[1], pairs[0]))


def open_sides():
    sides = []
    for axis in ("span", "pitch", "chord"):
        position, size = lax.axis_index(axis), lax.axis_size(axis)
        sides.append(jnp.where(position > 0, 1.0, 0.0).astype(jnp.float32))
        sides.append(jnp.where(position < size - 1, 1.0, 0.0).astype(jnp.float32))
    return sides


def sweep_kernel(
    table, start, source, classes, inner, y_low, y_high, x_out, z_low, z_high, p0, p1, p2, q, cs
):
    x_lo, x_hi, y_lo, y_hi, z_lo, z_hi = open_sides()
    shape = (GY, CZ)
    row, lane = iota(shape, 0), iota(shape, 1)
    keep = jnp.where(row < 8, y_lo, jnp.where(row >= 8 + CY, y_hi, 1.0))
    ends = (lane == 0) | (lane == CZ - 1)
    gate = jnp.where(lane == 0, z_lo, jnp.where(lane == CZ - 1, z_hi, 0.0))
    zeros = jnp.zeros(shape, jnp.float32)

    def clear(ref, planes):
        for c in range(3):
            for x in planes:
                ref[c, x] = zeros

    clear(p0, (2, 3, 20, 21))
    clear(p1, (1, 2, 21, 22))
    clear(p2, (0, 1, 22, 23))
    clear(q, (1, 2, 21, 22))
    clear(cs, (1, 2, 3, 20, 21, 22))

    def column(parts, x):
        total = zeros
        for c in range(3):
            total = total + pltpu.roll(jnp.where(ends, parts[c], 0.0), 2 * c + 1, 1)
        return pltpu.roll(total, 6 * (x - 2), 1)

    def across(ref, c, x):
        here = ref[c, x]
        planes = ref[c, x - 1] + ref[c, x + 1]
        lines = pltpu.roll(here, 1, 0) + pltpu.roll(here, GY - 1, 0)
        side = jnp.where(x < 4, x_lo, jnp.where(x >= 4 + CX, x_hi, 1.0))
        return here, (OWN * here + PULL[c][0] * planes + PULL[c][1] * lines) * (keep * side)

    def load(i, total):
        x = i + 4
        k = pick(table, classes[i])
        parts = []
        for c in range(3):
            for ref, value in ((p0, k * start[c, i]), (cs, STEP * source[c, i])):
                ref[c, x, 0:8, :] = jnp.zeros((8, CZ), jnp.float32)
                ref[c, x, 8 : 8 + CY, :] = value
                ref[c, x, 8 + CY : GY, :] = jnp.zeros((8, CZ), jnp.float32)
            parts.append(p0[c, x])
        return total + column(parts, x)

    col0 = lax.fori_loop(0, CX, load, zeros)

    def first(x, total):
        parts = []
        for c in range(3):
            here, flat = across(p0, c, x)
            new = flat + PULL[c][2] * shifted_lanes(here) + cs[c, x]
            p1[c, x] = new
            q[c, x] = flat + new
            parts.append(new)
        return total + column(parts, x)

    col1 = lax.fori_loop(3, 21, first, zeros)

    def second(x, total):
        parts = []
        for c in range(3):
            here, flat = across(p1, c, x)
            new = flat + PULL[c][2] * shifted_lanes(here) + cs[c, x]
            new = new + (PULL[c][2] * PULL[c][2] * gate) * p0[c, x]
            p2[c, x] = new
            parts.append(new)
        return total + column(parts, x)

    col2 = lax.fori_loop(2, 22, second, zeros)

    plane = (lane * 43) >> 8
    component = ((lane - 6 * plane) >> 1)
    lower = (lane & 1) == 1
    pull = [jnp.where(component == d, PULL[d][d], PULL[d][(d + 1) % 3]) for d in range(3)]
    side = jnp.where(plane < 2, x_lo, jnp.where(plane >= 2 + CX, x_hi, 1.0))
    side = jnp.where(lane < LANES, side, 0.0) * keep
    inside = jnp.where(lower, z_lo, z_hi)

    def flat_columns(v):
        planes = pltpu.roll(v, 6, 1) + pltpu.roll(v, CZ - 6, 1)
        lines = pltpu.roll(v, 1, 0) + pltpu.roll(v, GY - 1, 0)
        return (OWN * v + pull[0] * planes + pull[1] * lines) * side

    t1 = flat_columns(col0)
    out1 = inside * pull[2] * (
        flat_columns(t1) + flat_columns(col1) + col2 + pull[2] * pull[2] * col0
    )
    out2 = inside * pull[2] * pull[2] * (2.0 * t1 + col1)
    out3 = inside * pull[2] * pull[2] * pull[2] * col0
    z_low[0:GY, :] = jnp.where(lower, out1, pltpu.roll(out2, CZ - 1, 1))
    z_high[0:GY, :] = jnp.where(lower, pltpu.roll(out2, 1, 1), out1)
    near, far = out3[8:24, :], out3[24:40, :]
    half = lower[8:24, :]
    z_low[GY : GY + 16, :] = jnp.where(half, near, pltpu.roll(far, CZ - 1, 1))
    z_high[GY : GY + 16, :] = jnp.where(half, pltpu.roll(far, 1, 1), near)

    def third(x):
        values = []
        for c in range(3):
            here, flat = across(p2, c, x)
            new = flat + PULL[c][2] * shifted_lanes(here) + cs[c, x]
            new = new + (PULL[c][2] * PULL[c][2] * gate) * q[c, x]
            y_low[c, x] = new[0:8, :]
            y_high[c, x] = new[8 + CY : GY, :]
            values.append(new[8 : 8 + CY, :])
        return values

    for i, x in enumerate((1, 2, 3, 20, 21, 22)):
        for c, value in enumerate(third(x)):
            x_out[c, i] = value

    def middle(x, carry):
        for c, value in enumerate(third(x)):
            inner[c, x - 4] = value
        return carry

    lax.fori_loop(4, 20, middle, 0)


def chord_part(z_next, z_prev, c, x, start, size):
    lane = iota((size, CZ), 1)
    base = 6 * (x - 2) + 2 * c
    rows = slice(start, start + size)
    above = pltpu.roll(z_next[rows, :], (126 - base) % CZ, 1)
    below = pltpu.roll(z_prev[rows, :], (-base) % CZ, 1)
    return jnp.where(lane >= 126, above, jnp.where(lane < 2, below, 0.0))


def third_chord_part(z_next, z_prev, c, x, half):
    lane = iota((16, CZ), 1)
    base = 6 * (x - 2) + 2 * c
    above = pltpu.roll(z_next[GY : GY + 16, :], (124 + half - base) % CZ, 1)
    below = pltpu.roll(z_prev[GY : GY + 16, :], (2 - half - base) % CZ, 1)
    return jnp.where(lane == 125, above, jnp.where(lane == 2, below, 0.0))


def pitch_kernel(y_low, y_high, z_next, z_prev, low, high):
    for c in range(3):
        for x in range(1, 23):
            for tile, out, start, first in ((y_low, low, 0, 5), (y_high, high, 40, 0)):
                value = tile[c, x]
                if 2 <= x < 22:
                    value = value + chord_part(z_next, z_prev, c, x, start, 8)
                for j in range(3):
                    out[c, j, x : x + 1, :] = value[first + j : first + j + 1, :]


def pitch_rows(y_next, y_prev, c, x):
    row = iota((8, CZ), 0)
    bottom = jnp.zeros((8, CZ), jnp.float32)
    top = jnp.zeros((8, CZ), jnp.float32)
    for j in range(3):
        bottom = jnp.where(row == j, y_prev[c, j, x : x + 1, :], bottom)
        top = jnp.where(row == 5 + j, y_next[c, j, x : x + 1, :], top)
    return bottom, top


def span_kernel(x_out, z_next, z_prev, y_next, y_prev, low, high):
    for c in range(3):
        for i, x in enumerate((1, 2, 3, 20, 21, 22)):
            out, j = (low, i) if i < 3 else (high, i - 3)
            value = x_out[c, i]
            if 2 <= x < 22:
                value = value + chord_part(z_next, z_prev, c, x, 8, CY)
            out[c, j] = value
            bottom, top = pitch_rows(y_next, y_prev, c, x)
            out[c, j, 0:8, :] += bottom
            out[c, j, 24:32, :] += top


def wall_kernel(
    inverse, inner, classes, z_next, z_prev, y_next, y_prev, x_next, x_prev,
    wall_cell, patch_owner, wall_normal, mode_shape,
    adjoint, sums, plane_major, field,
):
    for x in range(CX):
        ratio = pick(inverse, classes[x])
        for c in range(3):
            value = inner[c, x] + chord_part(z_next, z_prev, c, x + 4, 8, CY)
            bottom, top = pitch_rows(y_next, y_prev, c, x + 4)
            near = third_chord_part(z_next, z_prev, c, x + 4, 0)
            far = third_chord_part(z_next, z_prev, c, x + 4, 1)
            zeros = jnp.zeros((8, CZ), jnp.float32)
            value = value + jnp.concatenate([near, far], axis=0)
            value = value + jnp.concatenate([bottom, zeros, zeros, top], axis=0)
            if x < 3:
                value = value + x_prev[c, x]
            if x >= CX - 3:
                value = value + x_next[c, x - (CX - 3)]
            adjoint[c, x] = value * ratio
            plane_major[c, CY * x : CY * (x + 1), :] = value

    for c in range(3):
        for g in range(4):
            block = plane_major[c, 128 * g : 128 * (g + 1), :].T
            first = block.astype(jnp.bfloat16)
            second = (block - first.astype(jnp.float32)).astype(jnp.bfloat16)
            field[256 * c : 256 * c + 128, 128 * g : 128 * (g + 1)] = first
            field[256 * c + 128 : 256 * c + 256, 128 * g : 128 * (g + 1)] = second

    def rows(step, total):
        here = pl.ds(pl.multiple_of(step * ROWS, ROWS), ROWS)
        cell, owner = wall_cell[:, here], patch_owner[:, here]
        planes = (iota((CX * CY, ROWS), 0) == (cell >> 7)).astype(jnp.bfloat16)
        picked = jnp.dot(field[...], planes, preferred_element_type=jnp.float32)
        value = jnp.zeros((CZ, ROWS), jnp.float32)
        for c in range(3):
            part = picked[256 * c : 256 * c + 128] + picked[256 * c + 128 : 256 * c + 256]
            value = value + wall_normal[c : c + 1, here] * part
        value = jnp.where(iota((CZ, ROWS), 0) == (cell & 127), value, 0.0)
        share = mode_shape[:, here] * jnp.sum(value, axis=0, keepdims=True)
        device = owner >> 7
        spread = jnp.concatenate([jnp.where(device == o, share, 0.0) for o in range(CHORD)], axis=0)
        first = spread.astype(jnp.bfloat16)
        second = (spread - first.astype(jnp.float32)).astype(jnp.bfloat16)
        patches = (iota((PATCH_DEV, ROWS), 0) == (owner & 127)).astype(jnp.bfloat16)
        both = jnp.concatenate([first, second], axis=0)
        return total + lax.dot_general(
            both, patches, (((1,), (1,)), ((), ())), preferred_element_type=jnp.float32
        )

    height = CHORD * MODES
    total = lax.fori_loop(0, WALL // ROWS, rows, jnp.zeros((2 * height, PATCH_DEV), jnp.float32))
    sums[...] = total[0:height] + total[height : 2 * height]


def call(kernel, outs, operands, scratch=(), smem=0, flops=0):
    shapes = tuple(jax.ShapeDtypeStruct(shape, jnp.float32) for shape in outs)
    moved = sum(4 * o.size for o in operands) + sum(4 * s.size for s in shapes)
    return pl.pallas_call(
        kernel,
        out_shape=shapes,
        in_specs=[SMEM] * smem + [VMEM] * (len(operands) - smem),
        out_specs=tuple(VMEM for _ in outs),
        scratch_shapes=list(scratch),
        cost_estimate=pl.CostEstimate(flops=flops, bytes_accessed=moved, transcendentals=0),
        compiler_params=pltpu.CompilerParams(vmem_limit_bytes=40 << 20),
    )(*operands)


def swap(low, high, axis):
    size = lax.axis_size(axis)
    up = [(i, i + 1) for i in range(size - 1)]
    down = [(j, i) for i, j in up]
    return lax.ppermute(low, axis, down), lax.ppermute(high, axis, up)


def body(
    adjoint_start,
    sensitivity_source,
    stiffness_class,
    stiffness_table,
    wall_cell,
    patch_owner,
    wall_normal,
    mode_shape,
):
    grown = pltpu.VMEM((3, GX, GY, CZ), jnp.float32)
    inner, y_low, y_high, x_out, z_low, z_high = call(
        sweep_kernel,
        ((3, CX, CY, CZ), (3, GX, 8, CZ), (3, GX, 8, CZ), (3, 6, CY, CZ), (GY + 16, CZ), (GY + 16, CZ)),
        (stiffness_table, adjoint_start, sensitivity_source, stiffness_class),
        scratch=(grown,) * 5,
        smem=1,
    )
    z_next, z_prev = swap(z_low, z_high, "chord")
    low, high = call(
        pitch_kernel, ((3, 3, GX, CZ), (3, 3, GX, CZ)), (y_low, y_high, z_next, z_prev)
    )
    y_next, y_prev = swap(low, high, "pitch")
    low, high = call(
        span_kernel, ((3, 3, CY, CZ), (3, 3, CY, CZ)), (x_out, z_next, z_prev, y_next, y_prev)
    )
    x_next, x_prev = swap(low, high, "span")
    adjoint, sums = call(
        wall_kernel,
        ((3, CX, CY, CZ), (CHORD * MODES, PATCH_DEV)),
        (
            1.0 / stiffness_table, inner, stiffness_class, z_next, z_prev, y_next, y_prev, x_next,
            x_prev, wall_cell.reshape(1, WALL), patch_owner.reshape(1, WALL), wall_normal, mode_shape,
        ),
        scratch=(
            pltpu.VMEM((3, CX * CY, CZ), jnp.float32),
            pltpu.VMEM((6 * CZ, CX * CY), jnp.bfloat16),
        ),
        smem=1,
    )
    sums = sums.reshape(CHORD, MODES, PATCH_DEV)
    arrived = lax.all_to_all(sums, "chord", split_axis=0, concat_axis=0, tiled=True)
    return adjoint, arrived.sum(axis=0)


def solution(mesh):
    in_specs = (
        P(None, "span", "pitch", "chord"),
        P(None, "span", "pitch", "chord"),
        P("span", "pitch", "chord"),
        P(),
        P(("span", "pitch", "chord")),
        P(("span", "pitch", "chord"), None),
        P(None, ("span", "pitch", "chord")),
        P(None, ("span", "pitch", "chord")),
    )
    out_specs = (P(None, "span", "pitch", "chord"), P(None, ("span", "pitch", "chord")))
    return jax.shard_map(body, mesh=mesh, in_specs=in_specs, out_specs=out_specs, check_vma=False)
```

```python
import functools

import jax
import jax.numpy as jnp
from jax import lax
from jax.experimental import pallas as pl
from jax.experimental.pallas import tpu as pltpu
from jax.sharding import PartitionSpec as P

CX, CY, CZ = 16, 32, 128
PATCH_DEV = 128
MODES = 8
CHORD = 16
WALL = 4096

MASS_SHIFT = 0.5
RELAXATION = 0.8
DIAGONAL_SUM = 10.5
LAME_WEIGHTS = ((3.0, 1.0, 1.0), (1.0, 3.0, 1.0), (1.0, 1.0, 3.0))

STEP = RELAXATION / DIAGONAL_SUM
OWN = 1.0 - STEP * (MASS_SHIFT + 2.0 * sum(LAME_WEIGHTS[0]))
PULL = tuple(tuple(STEP * weight for weight in row) for row in LAME_WEIGHTS)

GX, GY = 24, 48
FIRST, MIDDLE, LAST = 6, 24, 42
HALF = MIDDLE - FIRST
ROWS = 2048
STEP_X = 4

VMEM = pl.BlockSpec(memory_space=pltpu.VMEM)
SMEM = pl.BlockSpec(memory_space=pltpu.SMEM)
HBM = pl.BlockSpec(memory_space=pltpu.HBM)


def iota(shape, dim):
    return lax.broadcasted_iota(jnp.int32, shape, dim)


def shifted_lanes(v):
    lane = iota(v.shape, v.ndim - 1)
    before = jnp.where(lane == 0, 0.0, pltpu.roll(v, 1, v.ndim - 1))
    after = jnp.where(lane == CZ - 1, 0.0, pltpu.roll(v, CZ - 1, v.ndim - 1))
    return before + after


def pick(table, classes):
    low, mid, high = (classes & 1) == 1, (classes & 2) == 2, (classes & 4) == 4
    pairs = [jnp.where(low, table[2 * i + 1], table[2 * i]) for i in range(4)]
    return jnp.where(high, jnp.where(mid, pairs[3], pairs[2]), jnp.where(mid, pairs[1], pairs[0]))


def open_sides():
    sides = []
    for axis in ("span", "pitch", "chord"):
        position, size = lax.axis_index(axis), lax.axis_size(axis)
        sides.append(jnp.where(position > 0, 1.0, 0.0).astype(jnp.float32))
        sides.append(jnp.where(position < size - 1, 1.0, 0.0).astype(jnp.float32))
    return sides


def slots(shape):
    lane = iota(shape, len(shape) - 1)
    plane = (lane * 43) >> 8
    return plane, lane - 6 * plane


def column_kernel(
    table_in, start, source, classes, p0, cs, z_low, z_high,
    table, y_in, s_in, c_in, beyond, sems, table_sem,
):
    table_copy = pltpu.make_async_copy(table_in, table, table_sem)
    table_copy.start()
    copies = []
    for g in range(CX // STEP_X):
        part = pl.ds(g * STEP_X, STEP_X)
        copies.append(
            [
                pltpu.make_async_copy(classes.at[part], c_in.at[part], sems.at[0, g]),
                pltpu.make_async_copy(start.at[:, part], y_in.at[:, part], sems.at[1, g]),
                pltpu.make_async_copy(source.at[:, part], s_in.at[:, part], sems.at[2, g]),
            ]
        )
        for copy in copies[-1]:
            copy.start()
    x_lo, x_hi, y_lo, y_hi, z_lo, z_hi = open_sides()

    lane = iota((CY, CZ), 1)
    edge = (lane < 3) | (lane >= CZ - 3)
    values = [jnp.zeros((CY, CZ), jnp.float32) for _ in range(3)]
    pushes = [jnp.zeros((CY, CZ), jnp.float32) for _ in range(3)]
    table_copy.wait()
    for x in range(CX):
        if x % STEP_X == 0:
            for copy in copies[x // STEP_X]:
                copy.wait()
        k = pick(table, c_in[x])
        shift = (6 * (x + 2) + 3) % CZ
        for c in range(3):
            value = k * y_in[c, x]
            push = STEP * s_in[c, x]
            p0[c, x] = value
            cs[c, x] = push
            values[c] = values[c] + pltpu.roll(jnp.where(edge, value, 0.0), shift, 1)
            pushes[c] = pushes[c] + pltpu.roll(jnp.where(edge, push, 0.0), shift, 1)

    shape = (GY, CZ)
    plane, slot = slots(shape)
    row = iota(shape, 0)
    keep = jnp.where(row < 8, y_lo, jnp.where(row >= 8 + CY, y_hi, 1.0))
    side = jnp.where(plane < 2, x_lo, jnp.where(plane >= 2 + CX, x_hi, 1.0))
    side = jnp.where(plane < 20, side, 0.0) * keep
    at_high, at_low = slot == 2, slot == 3
    gate = jnp.where(at_high, z_hi, jnp.where(at_low, z_lo, 0.0))
    no_before, no_after = (slot == 0) | (slot == 3), (slot == 2) | (slot == 5)
    pad = jnp.zeros((8, CZ), jnp.float32)
    _, packed_slot = slots((HALF, CZ))

    for c in range(3):
        along = PULL[c][2]

        def flat(v):
            planes = pltpu.roll(v, 6, 1) + pltpu.roll(v, CZ - 6, 1)
            lines = pltpu.roll(v, 1, 0) + pltpu.roll(v, GY - 1, 0)
            return (OWN * v + PULL[c][0] * planes + PULL[c][1] * lines) * side

        def beside(v):
            before = jnp.where(no_before, 0.0, pltpu.roll(v, 1, 1))
            after = jnp.where(no_after, 0.0, pltpu.roll(v, CZ - 1, 1))
            return along * (before + after)

        v0 = jnp.concatenate([pad, values[c], pad], axis=0)
        push = jnp.concatenate([pad, pushes[c], pad], axis=0)
        t1 = flat(v0)
        v1 = t1 + beside(v0) + push
        t2 = flat(v1)
        v2 = t2 + beside(v1) + push + (along * along) * gate * v0
        out1 = along * gate * (flat(t1) + t2 + v2 + (along * along) * v0)
        out2 = (along * along) * gate * (2.0 * t1 + v1)
        out3 = (along * along * along) * gate * v0
        given = jnp.zeros(shape, jnp.float32)
        for far, out in ((1, out1), (2, out2), (3, out3)):
            given = given + pltpu.roll(jnp.where(at_low, out, 0.0), CZ - far, 1)
            given = given + pltpu.roll(jnp.where(at_high, out, 0.0), far, 1)
        beyond[c] = given
        top, rest = beyond[c, FIRST:MIDDLE, :], beyond[c, MIDDLE:LAST, :]
        rows = slice(HALF * c, HALF * (c + 1))
        z_low[rows, :] = jnp.where(packed_slot < 3, top, pltpu.roll(rest, 3, 1))
        z_high[rows, :] = jnp.where(packed_slot >= 3, rest, pltpu.roll(top, CZ - 3, 1))
    for out in (z_low, z_high):
        out[3 * HALF : 56, :] = jnp.zeros((56 - 3 * HALF, CZ), jnp.float32)


def sweep_kernel(p0_in, cs_in, inner, y_low, y_high, x_out, p0, p1, p2, q, cs):
    x_lo, x_hi, y_lo, y_hi, z_lo, z_hi = open_sides()
    shape = (GY, CZ)
    row, lane = iota(shape, 0), iota(shape, 1)
    keep = jnp.where(row < 8, y_lo, jnp.where(row >= 8 + CY, y_hi, 1.0))
    gate = jnp.where(lane == 0, z_lo, jnp.where(lane == CZ - 1, z_hi, 0.0))
    zeros = jnp.zeros(shape, jnp.float32)

    def clear(ref, planes):
        for c in range(3):
            for x in planes:
                ref[c, x] = zeros

    clear(p0, (2, 3, 20, 21))
    clear(p1, (1, 2, 21, 22))
    clear(p2, (0, 1, 22, 23))
    clear(q, (1, 2, 21, 22))
    clear(cs, (1, 2, 3, 20, 21, 22))
    pad = jnp.zeros((8, CZ), jnp.float32)
    for x in range(CX):
        for c in range(3):
            for ref, given in ((p0, p0_in), (cs, cs_in)):
                ref[c, x + 4, 0:8, :] = pad
                ref[c, x + 4, 8 : 8 + CY, :] = given[c, x]
                ref[c, x + 4, 8 + CY : GY, :] = pad

    def across(ref, c, x):
        here = ref[c, x]
        planes = ref[c, x - 1] + ref[c, x + 1]
        lines = pltpu.roll(here, 1, 0) + pltpu.roll(here, GY - 1, 0)
        side = jnp.where(x < 4, x_lo, jnp.where(x >= 4 + CX, x_hi, 1.0))
        return here, (OWN * here + PULL[c][0] * planes + PULL[c][1] * lines) * (keep * side)

    def first(x, carry):
        for c in range(3):
            here, flat = across(p0, c, x)
            new = flat + PULL[c][2] * shifted_lanes(here) + cs[c, x]
            p1[c, x] = new
            q[c, x] = flat + new
        return carry

    lax.fori_loop(3, 21, first, 0, unroll=True)

    def second(x, carry):
        for c in range(3):
            here, flat = across(p1, c, x)
            new = flat + PULL[c][2] * shifted_lanes(here) + cs[c, x]
            p2[c, x] = new + (PULL[c][2] * PULL[c][2] * gate) * p0[c, x]
        return carry

    lax.fori_loop(2, 22, second, 0, unroll=True)

    def third(x):
        values = []
        for c in range(3):
            here, flat = across(p2, c, x)
            new = flat + PULL[c][2] * shifted_lanes(here) + cs[c, x]
            new = new + (PULL[c][2] * PULL[c][2] * gate) * q[c, x]
            y_low[c, x] = new[0:8, :]
            y_high[c, x] = new[8 + CY : GY, :]
            values.append(new[8 : 8 + CY, :])
        return values

    for i, x in enumerate((1, 2, 3, 20, 21, 22)):
        for c, value in enumerate(third(x)):
            x_out[c, i] = value

    def middle(x, carry):
        for c, value in enumerate(third(x)):
            inner[c, x - 4] = value
        return carry

    lax.fori_loop(4, 20, middle, 0, unroll=True)


def unpack(z_next, z_prev, columns):
    _, slot = slots((HALF, CZ))
    for c in range(3):
        rows = slice(HALF * c, HALF * (c + 1))
        above, below = z_next[rows, :], z_prev[rows, :]
        columns[c, 0:8, :] = jnp.zeros((8, CZ), jnp.float32)
        columns[c, GY - 8 : GY, :] = jnp.zeros((8, CZ), jnp.float32)
        columns[c, FIRST:MIDDLE, :] = jnp.where(slot < 3, above, pltpu.roll(below, 3, 1))
        columns[c, MIDDLE:LAST, :] = jnp.where(slot < 3, pltpu.roll(above, CZ - 3, 1), below)


def chord_part(columns, c, x, start, size):
    lane = iota((size, CZ), 1)
    placed = pltpu.roll(columns[c, start : start + size, :], (CZ - 3 - 6 * (x - 2)) % CZ, 1)
    return jnp.where((lane < 3) | (lane >= CZ - 3), placed, 0.0)


def pitch_kernel(y_low, y_high, z_next, z_prev, low, high, columns):
    unpack(z_next, z_prev, columns)
    for c in range(3):
        for x in range(1, 23):
            for tile, out, start, first in ((y_low, low, 0, 5), (y_high, high, 40, 0)):
                value = tile[c, x]
                if 2 <= x < 22:
                    value = value + chord_part(columns, c, x, start, 8)
                for j in range(3):
                    out[c, j, x : x + 1, :] = value[first + j : first + j + 1, :]


def pitch_rows(y_next, y_prev, c, x):
    row = iota((8, CZ), 0)
    bottom = jnp.zeros((8, CZ), jnp.float32)
    top = jnp.zeros((8, CZ), jnp.float32)
    for j in range(3):
        bottom = jnp.where(row == j, y_prev[c, j, x : x + 1, :], bottom)
        top = jnp.where(row == 5 + j, y_next[c, j, x : x + 1, :], top)
    return bottom, top


def span_kernel(x_out, z_next, z_prev, y_next, y_prev, low, high, columns):
    unpack(z_next, z_prev, columns)
    for c in range(3):
        for i, x in enumerate((1, 2, 3, 20, 21, 22)):
            out, j = (low, i) if i < 3 else (high, i - 3)
            value = x_out[c, i]
            if 2 <= x < 22:
                value = value + chord_part(columns, c, x, 8, CY)
            out[c, j] = value
            bottom, top = pitch_rows(y_next, y_prev, c, x)
            out[c, j, 0:8, :] += bottom
            out[c, j, 24:32, :] += top


def finish_planes(planes, inner, z_next, z_prev, y_next, y_prev, ratio_of, columns, values, part, field, span):
    unpack(z_next, z_prev, columns)
    zeros = jnp.zeros((8, CZ), jnp.float32)
    for i, x in enumerate(planes):
        ratio = ratio_of(x)
        for c in range(3):
            value = inner[c, x] + chord_part(columns, c, x + 4, 8, CY)
            bottom, top = pitch_rows(y_next, y_prev, c, x + 4)
            value = value + jnp.concatenate([bottom, zeros, zeros, top], axis=0)
            value = span(value, c, x)
            values[c, i] = value * ratio
            part[c, CY * i : CY * (i + 1), :] = value
    for c in range(3):
        for g in range(CY * len(planes) // 128):
            block = part[c, 128 * g : 128 * (g + 1), :].T
            first = block.astype(jnp.bfloat16)
            second = (block - first.astype(jnp.float32)).astype(jnp.bfloat16)
            field[256 * c : 256 * c + 128, 128 * g : 128 * (g + 1)] = first
            field[256 * c + 128 : 256 * c + 256, 128 * g : 128 * (g + 1)] = second


def normal_share(field, place, cell, normals):
    count = place.shape[1]
    planes = (iota((field.shape[1], count), 0) == place).astype(jnp.bfloat16)
    picked = jnp.dot(field[...], planes, preferred_element_type=jnp.float32)
    value = jnp.zeros((CZ, count), jnp.float32)
    for c in range(3):
        part = picked[256 * c : 256 * c + 128] + picked[256 * c + 128 : 256 * c + 256]
        value = value + normals[c : c + 1] * part
    value = jnp.where(iota((CZ, count), 0) == (cell & 127), value, 0.0)
    return jnp.sum(value, axis=0, keepdims=True)


def middle_kernel(
    inverse, inner, classes, z_next, z_prev, y_next, y_prev, wall_cell, wall_normal,
    adjoint, share, columns, values, part, field, sem,
):
    def as_is(value, c, x):
        return value

    finish_planes(
        range(4, 12), inner, z_next, z_prev, y_next, y_prev,
        lambda x: pick(inverse, classes[x]), columns, values, part, field, as_is,
    )
    copy = pltpu.make_async_copy(values, adjoint.at[:, 4:12], sem)
    copy.start()
    for step in range(WALL // ROWS):
        here = slice(step * ROWS, (step + 1) * ROWS)
        cell = wall_cell[:, here]
        share[:, here] = normal_share(field, (cell >> 7) - 128, cell, wall_normal[:, here])
    copy.wait()


def wall_kernel(
    inverse, given, inner, classes, z_next, z_prev, y_next, y_prev, x_next, x_prev, share,
    wall_cell, patch_owner, wall_normal, mode_shape,
    adjoint, sums, columns, values, part, field, sems,
):
    def span(value, c, x):
        if x < 3:
            return value + x_prev[c, x]
        if x >= CX - 3:
            return value + x_next[c, x - (CX - 3)]
        return value

    finish_planes(
        (0, 1, 2, 3, 12, 13, 14, 15), inner, z_next, z_prev, y_next, y_prev,
        lambda x: pick(inverse, classes[x]), columns, values, part, field, span,
    )
    copies = [
        pltpu.make_async_copy(values.at[:, 0:4], adjoint.at[:, 0:4], sems.at[0]),
        pltpu.make_async_copy(values.at[:, 4:8], adjoint.at[:, 12:16], sems.at[1]),
    ]
    for copy in copies:
        copy.start()
    height = CHORD * MODES
    total = jnp.zeros((2 * height, PATCH_DEV), jnp.float32)
    for step in range(WALL // ROWS):
        here = slice(step * ROWS, (step + 1) * ROWS)
        cell, owner = wall_cell[:, here], patch_owner[:, here]
        plane = cell >> 7
        place = jnp.where(plane < 128, plane, jnp.where(plane >= 384, plane - 256, -1))
        normal = share[:, here] + normal_share(field, place, cell, wall_normal[:, here])
        parts = mode_shape[:, here] * normal
        device = owner >> 7
        spread = jnp.concatenate([jnp.where(device == o, parts, 0.0) for o in range(CHORD)], axis=0)
        first = spread.astype(jnp.bfloat16)
        second = (spread - first.astype(jnp.float32)).astype(jnp.bfloat16)
        patches = (iota((PATCH_DEV, ROWS), 0) == (owner & 127)).astype(jnp.bfloat16)
        both = jnp.concatenate([first, second], axis=0)
        total = total + lax.dot_general(
            both, patches, (((1,), (1,)), ((), ())), preferred_element_type=jnp.float32
        )
    sums[...] = total[0:height] + total[height : 2 * height]
    for copy in copies:
        copy.wait()


def call(kernel, outs, operands, spaces, scratch=(), out_spaces=None, aliases=None, flops=0):
    spec = {"h": HBM, "s": SMEM, "v": VMEM}
    shapes = tuple(jax.ShapeDtypeStruct(shape, jnp.float32) for shape in outs)
    moved = sum(4 * o.size for o in operands) + sum(4 * s.size for s in shapes)
    operands = [
        pltpu.with_memory_space_constraint(o, pltpu.HBM) if space == "h" else o
        for o, space in zip(operands, spaces)
    ]
    return pl.pallas_call(
        kernel,
        out_shape=shapes,
        in_specs=[spec[space] for space in spaces],
        out_specs=tuple(spec[space] for space in out_spaces or "v" * len(outs)),
        scratch_shapes=list(scratch),
        input_output_aliases=aliases or {},
        cost_estimate=pl.CostEstimate(flops=flops, bytes_accessed=moved, transcendentals=0),
        compiler_params=pltpu.CompilerParams(vmem_limit_bytes=40 << 20),
    )(*operands)


def swap(low, high, axis):
    size = lax.axis_size(axis)
    up = [(i, i + 1) for i in range(size - 1)]
    down = [(j, i) for i, j in up]
    return lax.ppermute(low, axis, down), lax.ppermute(high, axis, up)


def body(
    adjoint_start,
    sensitivity_source,
    stiffness_class,
    stiffness_table,
    wall_cell,
    patch_owner,
    wall_normal,
    mode_shape,
):
    block, columns = (3, CX, CY, CZ), pltpu.VMEM((3, GY, CZ), jnp.float32)
    grown = pltpu.VMEM((3, GX, GY, CZ), jnp.float32)
    p0, cs, z_low, z_high = call(
        column_kernel,
        (block, block, (56, CZ), (56, CZ)),
        (stiffness_table, adjoint_start, sensitivity_source, stiffness_class),
        "hhhh",
        scratch=(
            pltpu.SMEM((8,), jnp.float32),
            pltpu.VMEM(block, jnp.float32),
            pltpu.VMEM(block, jnp.float32),
            pltpu.VMEM((CX, CY, CZ), jnp.int32),
            columns,
            pltpu.SemaphoreType.DMA((3, CX // STEP_X)),
            pltpu.SemaphoreType.DMA,
        ),
    )
    z_next, z_prev = swap(z_low, z_high, "chord")
    inner, y_low, y_high, x_out = call(
        sweep_kernel,
        (block, (3, GX, 8, CZ), (3, GX, 8, CZ), (3, 6, CY, CZ)),
        (p0, cs),
        "vv",
        scratch=(grown,) * 5,
        flops=1 << 25,
    )
    slab = (3, 3, GX, CZ)
    low, high = call(
        pitch_kernel, (slab, slab), (y_low, y_high, z_next, z_prev), "vvvv", scratch=(columns,)
    )
    y_next, y_prev = swap(low, high, "pitch")
    slab = (3, 3, CY, CZ)
    low, high = call(
        span_kernel, (slab, slab), (x_out, z_next, z_prev, y_next, y_prev), "vvvvv", scratch=(columns,)
    )
    x_next, x_prev = swap(low, high, "span")
    inverse, cells = 1.0 / stiffness_table, wall_cell.reshape(1, WALL)
    given = (z_next, z_prev, y_next, y_prev)
    work = (
        columns,
        pltpu.VMEM((3, CX // 2, CY, CZ), jnp.float32),
        pltpu.VMEM((3, CX // 2 * CY, CZ), jnp.float32),
        pltpu.VMEM((6 * CZ, CX // 2 * CY), jnp.bfloat16),
    )
    adjoint, share = call(
        middle_kernel,
        (block, (1, WALL)),
        (inverse, inner, stiffness_class, *given, cells, wall_normal),
        "svvvvvvvv",
        scratch=(*work, pltpu.SemaphoreType.DMA),
        out_spaces="hv",
        flops=1 << 30,
    )
    adjoint, sums = call(
        wall_kernel,
        (block, (CHORD * MODES, PATCH_DEV)),
        (
            inverse, adjoint, inner, stiffness_class, *given, x_next, x_prev, share,
            cells, patch_owner.reshape(1, WALL), wall_normal, mode_shape,
        ),
        "shvvvvvvvvvvvvv",
        scratch=(*work, pltpu.SemaphoreType.DMA((2,))),
        out_spaces="hv",
        aliases={1: 0},
        flops=1 << 30,
    )
    sums = sums.reshape(CHORD, MODES, PATCH_DEV)
    arrived = lax.all_to_all(sums, "chord", split_axis=0, concat_axis=0, tiled=True)
    return adjoint, arrived.sum(axis=0)


def solution(mesh):
    in_specs = (
        P(None, "span", "pitch", "chord"),
        P(None, "span", "pitch", "chord"),
        P("span", "pitch", "chord"),
        P(),
        P(("span", "pitch", "chord")),
        P(("span", "pitch", "chord"), None),
        P(None, ("span", "pitch", "chord")),
        P(None, ("span", "pitch", "chord")),
    )
    out_specs = (P(None, "span", "pitch", "chord"), P(None, ("span", "pitch", "chord")))
    return jax.shard_map(body, mesh=mesh, in_specs=in_specs, out_specs=out_specs, check_vma=False)
```

```python
import functools

import jax
import jax.numpy as jnp
from jax import lax
from jax.experimental import pallas as pl
from jax.experimental.pallas import tpu as pltpu
from jax.sharding import PartitionSpec as P

CX, CY, CZ = 16, 32, 128
PATCH_DEV = 128
MODES = 8
CHORD = 16
WALL = 4096

MASS_SHIFT = 0.5
RELAXATION = 0.8
DIAGONAL_SUM = 10.5
LAME_WEIGHTS = ((3.0, 1.0, 1.0), (1.0, 3.0, 1.0), (1.0, 1.0, 3.0))

STEP = RELAXATION / DIAGONAL_SUM
OWN = 1.0 - STEP * (MASS_SHIFT + 2.0 * sum(LAME_WEIGHTS[0]))
PULL = tuple(tuple(STEP * weight for weight in row) for row in LAME_WEIGHTS)

GX, GY = 24, 48
FIRST, MIDDLE, LAST = 6, 24, 42
HALF = MIDDLE - FIRST
ROWS = 2048
STEP_X = 4

VMEM = pl.BlockSpec(memory_space=pltpu.VMEM)
SMEM = pl.BlockSpec(memory_space=pltpu.SMEM)
HBM = pl.BlockSpec(memory_space=pltpu.HBM)


def iota(shape, dim):
    return lax.broadcasted_iota(jnp.int32, shape, dim)


def shifted_lanes(v):
    lane = iota(v.shape, v.ndim - 1)
    before = jnp.where(lane == 0, 0.0, pltpu.roll(v, 1, v.ndim - 1))
    after = jnp.where(lane == CZ - 1, 0.0, pltpu.roll(v, CZ - 1, v.ndim - 1))
    return before + after


def pick(table, classes):
    low, mid, high = (classes & 1) == 1, (classes & 2) == 2, (classes & 4) == 4
    pairs = [jnp.where(low, table[2 * i + 1], table[2 * i]) for i in range(4)]
    return jnp.where(high, jnp.where(mid, pairs[3], pairs[2]), jnp.where(mid, pairs[1], pairs[0]))


def open_sides():
    sides = []
    for axis in ("span", "pitch", "chord"):
        position, size = lax.axis_index(axis), lax.axis_size(axis)
        sides.append(jnp.where(position > 0, 1.0, 0.0).astype(jnp.float32))
        sides.append(jnp.where(position < size - 1, 1.0, 0.0).astype(jnp.float32))
    return sides


def slots(shape):
    lane = iota(shape, len(shape) - 1)
    plane = (lane * 43) >> 8
    return plane, lane - 6 * plane


def column_kernel(
    table_in, start, source, classes, p0, cs, stiffness, z_low, z_high,
    table, y_in, s_in, c_in, beyond, sems, table_sem,
):
    table_copy = pltpu.make_async_copy(table_in, table, table_sem)
    table_copy.start()
    copies = []
    for g in range(CX // STEP_X):
        part = pl.ds(g * STEP_X, STEP_X)
        copies.append(
            [
                pltpu.make_async_copy(classes.at[part], c_in.at[part], sems.at[0, g]),
                pltpu.make_async_copy(start.at[:, part], y_in.at[:, part], sems.at[1, g]),
                pltpu.make_async_copy(source.at[:, part], s_in.at[:, part], sems.at[2, g]),
            ]
        )
        for copy in copies[-1]:
            copy.start()
    x_lo, x_hi, y_lo, y_hi, z_lo, z_hi = open_sides()

    lane = iota((CY, CZ), 1)
    edge = (lane < 3) | (lane >= CZ - 3)
    values = [jnp.zeros((CY, CZ), jnp.float32) for _ in range(3)]
    pushes = [jnp.zeros((CY, CZ), jnp.float32) for _ in range(3)]
    table_copy.wait()
    for x in range(CX):
        if x % STEP_X == 0:
            for copy in copies[x // STEP_X]:
                copy.wait()
        k = pick(table, c_in[x])
        stiffness[x] = k
        shift = (6 * (x + 2) + 3) % CZ
        for c in range(3):
            value = k * y_in[c, x]
            push = STEP * s_in[c, x]
            p0[c, x] = value
            cs[c, x] = push
            values[c] = values[c] + pltpu.roll(jnp.where(edge, value, 0.0), shift, 1)
            pushes[c] = pushes[c] + pltpu.roll(jnp.where(edge, push, 0.0), shift, 1)

    shape = (GY, CZ)
    plane, slot = slots(shape)
    row = iota(shape, 0)
    keep = jnp.where(row < 8, y_lo, jnp.where(row >= 8 + CY, y_hi, 1.0))
    side = jnp.where(plane < 2, x_lo, jnp.where(plane >= 2 + CX, x_hi, 1.0))
    side = jnp.where(plane < 20, side, 0.0) * keep
    at_high, at_low = slot == 2, slot == 3
    gate = jnp.where(at_high, z_hi, jnp.where(at_low, z_lo, 0.0))
    no_before, no_after = (slot == 0) | (slot == 3), (slot == 2) | (slot == 5)
    pad = jnp.zeros((8, CZ), jnp.float32)
    _, packed_slot = slots((HALF, CZ))

    for c in range(3):
        along = PULL[c][2]

        def flat(v):
            planes = pltpu.roll(v, 6, 1) + pltpu.roll(v, CZ - 6, 1)
            lines = pltpu.roll(v, 1, 0) + pltpu.roll(v, GY - 1, 0)
            return (OWN * v + PULL[c][0] * planes + PULL[c][1] * lines) * side

        def beside(v):
            before = jnp.where(no_before, 0.0, pltpu.roll(v, 1, 1))
            after = jnp.where(no_after, 0.0, pltpu.roll(v, CZ - 1, 1))
            return along * (before + after)

        v0 = jnp.concatenate([pad, values[c], pad], axis=0)
        push = jnp.concatenate([pad, pushes[c], pad], axis=0)
        t1 = flat(v0)
        v1 = t1 + beside(v0) + push
        t2 = flat(v1)
        v2 = t2 + beside(v1) + push + (along * along) * gate * v0
        out1 = along * gate * (flat(t1) + t2 + v2 + (along * along) * v0)
        out2 = (along * along) * gate * (2.0 * t1 + v1)
        out3 = (along * along * along) * gate * v0
        given = jnp.zeros(shape, jnp.float32)
        for far, out in ((1, out1), (2, out2), (3, out3)):
            given = given + pltpu.roll(jnp.where(at_low, out, 0.0), CZ - far, 1)
            given = given + pltpu.roll(jnp.where(at_high, out, 0.0), far, 1)
        beyond[c] = given
        top, rest = beyond[c, FIRST:MIDDLE, :], beyond[c, MIDDLE:LAST, :]
        rows = slice(HALF * c, HALF * (c + 1))
        z_low[rows, :] = jnp.where(packed_slot < 3, top, pltpu.roll(rest, 3, 1))
        z_high[rows, :] = jnp.where(packed_slot >= 3, rest, pltpu.roll(top, CZ - 3, 1))
    for out in (z_low, z_high):
        out[3 * HALF : 56, :] = jnp.zeros((56 - 3 * HALF, CZ), jnp.float32)


def sweep_kernel(p0_in, cs_in, inner, y_low, y_high, x_out, p0, p1, p2, q, cs):
    x_lo, x_hi, y_lo, y_hi, z_lo, z_hi = open_sides()
    shape = (GY, CZ)
    row, lane = iota(shape, 0), iota(shape, 1)
    keep = jnp.where(row < 8, y_lo, jnp.where(row >= 8 + CY, y_hi, 1.0))
    gate = jnp.where(lane == 0, z_lo, jnp.where(lane == CZ - 1, z_hi, 0.0))
    zeros = jnp.zeros(shape, jnp.float32)

    def clear(ref, planes):
        for c in range(3):
            for x in planes:
                ref[c, x] = zeros

    clear(p0, (2, 3, 20, 21))
    clear(p1, (1, 2, 21, 22))
    clear(p2, (0, 1, 22, 23))
    clear(q, (1, 2, 21, 22))
    clear(cs, (1, 2, 3, 20, 21, 22))
    pad = jnp.zeros((8, CZ), jnp.float32)
    for x in range(CX):
        for c in range(3):
            for ref, given in ((p0, p0_in), (cs, cs_in)):
                ref[c, x + 4, 0:8, :] = pad
                ref[c, x + 4, 8 : 8 + CY, :] = given[c, x]
                ref[c, x + 4, 8 + CY : GY, :] = pad

    def across(ref, c, x):
        here = ref[c, x]
        planes = ref[c, x - 1] + ref[c, x + 1]
        lines = pltpu.roll(here, 1, 0) + pltpu.roll(here, GY - 1, 0)
        side = jnp.where(x < 4, x_lo, jnp.where(x >= 4 + CX, x_hi, 1.0))
        return here, (OWN * here + PULL[c][0] * planes + PULL[c][1] * lines) * (keep * side)

    def first(x, carry):
        for c in range(3):
            here, flat = across(p0, c, x)
            new = flat + PULL[c][2] * shifted_lanes(here) + cs[c, x]
            p1[c, x] = new
            q[c, x] = flat + new
        return carry

    lax.fori_loop(3, 21, first, 0, unroll=True)

    def second(x, carry):
        for c in range(3):
            here, flat = across(p1, c, x)
            new = flat + PULL[c][2] * shifted_lanes(here) + cs[c, x]
            p2[c, x] = new + (PULL[c][2] * PULL[c][2] * gate) * p0[c, x]
        return carry

    lax.fori_loop(2, 22, second, 0, unroll=True)

    def third(x):
        values = []
        for c in range(3):
            here, flat = across(p2, c, x)
            new = flat + PULL[c][2] * shifted_lanes(here) + cs[c, x]
            new = new + (PULL[c][2] * PULL[c][2] * gate) * q[c, x]
            y_low[c, x] = new[0:8, :]
            y_high[c, x] = new[8 + CY : GY, :]
            values.append(new[8 : 8 + CY, :])
        return values

    for i, x in enumerate((1, 2, 3, 20, 21, 22)):
        for c, value in enumerate(third(x)):
            x_out[c, i] = value

    def middle(x, carry):
        for c, value in enumerate(third(x)):
            inner[c, x - 4] = value
        return carry

    lax.fori_loop(4, 20, middle, 0, unroll=True)


def unpack(z_next, z_prev, columns):
    _, slot = slots((HALF, CZ))
    for c in range(3):
        rows = slice(HALF * c, HALF * (c + 1))
        above, below = z_next[rows, :], z_prev[rows, :]
        columns[c, 0:8, :] = jnp.zeros((8, CZ), jnp.float32)
        columns[c, GY - 8 : GY, :] = jnp.zeros((8, CZ), jnp.float32)
        columns[c, FIRST:MIDDLE, :] = jnp.where(slot < 3, above, pltpu.roll(below, 3, 1))
        columns[c, MIDDLE:LAST, :] = jnp.where(slot < 3, pltpu.roll(above, CZ - 3, 1), below)


def chord_part(columns, c, x, start, size):
    lane = iota((size, CZ), 1)
    placed = pltpu.roll(columns[c, start : start + size, :], (CZ - 3 - 6 * (x - 2)) % CZ, 1)
    return jnp.where((lane < 3) | (lane >= CZ - 3), placed, 0.0)


def pitch_kernel(y_low, y_high, z_next, z_prev, low, high, columns):
    unpack(z_next, z_prev, columns)
    for c in range(3):
        for x in range(1, 23):
            for tile, out, start, first in ((y_low, low, 0, 5), (y_high, high, 40, 0)):
                value = tile[c, x]
                if 2 <= x < 22:
                    value = value + chord_part(columns, c, x, start, 8)
                for j in range(3):
                    out[c, j, x : x + 1, :] = value[first + j : first + j + 1, :]


def pitch_rows(y_next, y_prev, c, x):
    row = iota((8, CZ), 0)
    bottom = jnp.zeros((8, CZ), jnp.float32)
    top = jnp.zeros((8, CZ), jnp.float32)
    for j in range(3):
        bottom = jnp.where(row == j, y_prev[c, j, x : x + 1, :], bottom)
        top = jnp.where(row == 5 + j, y_next[c, j, x : x + 1, :], top)
    return bottom, top


def span_kernel(x_out, z_next, z_prev, y_next, y_prev, low, high, columns):
    unpack(z_next, z_prev, columns)
    for c in range(3):
        for i, x in enumerate((1, 2, 3, 20, 21, 22)):
            out, j = (low, i) if i < 3 else (high, i - 3)
            value = x_out[c, i]
            if 2 <= x < 22:
                value = value + chord_part(columns, c, x, 8, CY)
            out[c, j] = value
            bottom, top = pitch_rows(y_next, y_prev, c, x)
            out[c, j, 0:8, :] += bottom
            out[c, j, 24:32, :] += top


def finish_planes(planes, inner, z_next, z_prev, y_next, y_prev, stiffness, columns, values, part, field, span):
    unpack(z_next, z_prev, columns)
    zeros = jnp.zeros((8, CZ), jnp.float32)
    for i, x in enumerate(planes):
        ratio = 1.0 / stiffness[x]
        for c in range(3):
            value = inner[c, x] + chord_part(columns, c, x + 4, 8, CY)
            bottom, top = pitch_rows(y_next, y_prev, c, x + 4)
            value = value + jnp.concatenate([bottom, zeros, zeros, top], axis=0)
            value = span(value, c, x)
            values[c, i] = value * ratio
            part[c, CY * i : CY * (i + 1), :] = value
    for c in range(3):
        for g in range(CY * len(planes) // 128):
            block = part[c, 128 * g : 128 * (g + 1), :].T
            first = block.astype(jnp.bfloat16)
            second = (block - first.astype(jnp.float32)).astype(jnp.bfloat16)
            field[256 * c : 256 * c + 128, 128 * g : 128 * (g + 1)] = first
            field[256 * c + 128 : 256 * c + 256, 128 * g : 128 * (g + 1)] = second


def marks(length, place):
    return (iota((length, place.shape[1]), 0) == place).astype(jnp.bfloat16)


def mark_kernel(wall_cell, patch_owner, after, planes, patches):
    for step in range(WALL // 512):
        here = slice(step * 512, (step + 1) * 512)
        plane = wall_cell[:, here] >> 7
        place = jnp.where(plane < 128, plane, jnp.where(plane >= 384, plane - 256, -1))
        planes[:, here] = marks(256, place)
        patches[here, :] = marks(PATCH_DEV, patch_owner[:, here] & 127).T


def normal_share(field, planes, cell, normals):
    count = cell.shape[1]
    picked = jnp.dot(field[...], planes, preferred_element_type=jnp.float32)
    value = jnp.zeros((CZ, count), jnp.float32)
    for c in range(3):
        part = picked[256 * c : 256 * c + 128] + picked[256 * c + 128 : 256 * c + 256]
        value = value + normals[c : c + 1] * part
    value = jnp.where(iota((CZ, count), 0) == (cell & 127), value, 0.0)
    return jnp.sum(value, axis=0, keepdims=True)


def middle_kernel(
    inner, stiffness, z_next, z_prev, y_next, y_prev, wall_cell, wall_normal,
    adjoint, share, columns, values, part, field, sem,
):
    def as_is(value, c, x):
        return value

    finish_planes(
        range(4, 12), inner, z_next, z_prev, y_next, y_prev,
        stiffness, columns, values, part, field, as_is,
    )
    copy = pltpu.make_async_copy(values, adjoint.at[:, 4:12], sem)
    copy.start()
    for step in range(WALL // ROWS):
        here = slice(step * ROWS, (step + 1) * ROWS)
        cell = wall_cell[:, here]
        share[:, here] = normal_share(
            field, marks(256, (cell >> 7) - 128), cell, wall_normal[:, here]
        )
    copy.wait()


def wall_kernel(
    given, inner, stiffness, z_next, z_prev, y_next, y_prev, x_next, x_prev, share,
    wall_cell, patch_owner, wall_normal, mode_shape, planes, patches,
    adjoint, sums, columns, values, part, field, sems,
):
    def span(value, c, x):
        if x < 3:
            return value + x_prev[c, x]
        if x >= CX - 3:
            return value + x_next[c, x - (CX - 3)]
        return value

    finish_planes(
        (0, 1, 2, 3, 12, 13, 14, 15), inner, z_next, z_prev, y_next, y_prev,
        stiffness, columns, values, part, field, span,
    )
    copies = [
        pltpu.make_async_copy(values.at[:, 0:4], adjoint.at[:, 0:4], sems.at[0]),
        pltpu.make_async_copy(values.at[:, 4:8], adjoint.at[:, 12:16], sems.at[1]),
    ]
    for copy in copies:
        copy.start()
    height = CHORD * MODES
    total = jnp.zeros((2 * height, PATCH_DEV), jnp.float32)
    for step in range(WALL // ROWS):
        here = slice(step * ROWS, (step + 1) * ROWS)
        cell, owner = wall_cell[:, here], patch_owner[:, here]
        normal = share[:, here] + normal_share(field, planes[:, here], cell, wall_normal[:, here])
        parts = mode_shape[:, here] * normal
        device = owner >> 7
        spread = jnp.concatenate([jnp.where(device == o, parts, 0.0) for o in range(CHORD)], axis=0)
        first = spread.astype(jnp.bfloat16)
        second = (spread - first.astype(jnp.float32)).astype(jnp.bfloat16)
        both = jnp.concatenate([first, second], axis=0)
        total = total + jnp.dot(both, patches[here, :], preferred_element_type=jnp.float32)
    sums[...] = total[0:height] + total[height : 2 * height]
    for copy in copies:
        copy.wait()


def call(
    kernel, outs, operands, spaces, scratch=(), out_spaces=None, aliases=None, flops=0, kind=jnp.float32
):
    spec = {"h": HBM, "s": SMEM, "v": VMEM}
    shapes = tuple(jax.ShapeDtypeStruct(shape, kind) for shape in outs)
    moved = sum(4 * o.size for o in operands) + sum(4 * s.size for s in shapes)
    operands = [
        pltpu.with_memory_space_constraint(o, pltpu.HBM) if space == "h" else o
        for o, space in zip(operands, spaces)
    ]
    return pl.pallas_call(
        kernel,
        out_shape=shapes,
        in_specs=[spec[space] for space in spaces],
        out_specs=tuple(spec[space] for space in out_spaces or "v" * len(outs)),
        scratch_shapes=list(scratch),
        input_output_aliases=aliases or {},
        cost_estimate=pl.CostEstimate(flops=flops, bytes_accessed=moved, transcendentals=0),
        compiler_params=pltpu.CompilerParams(vmem_limit_bytes=40 << 20),
    )(*operands)


def pairs(axis):
    return [(i, i + 1) for i in range(lax.axis_size(axis) - 1)]


def from_next(low, axis):
    return lax.ppermute(low, axis, [(j, i) for i, j in pairs(axis)])


def from_previous(high, axis):
    return lax.ppermute(high, axis, pairs(axis))


def body(
    adjoint_start,
    sensitivity_source,
    stiffness_class,
    stiffness_table,
    wall_cell,
    patch_owner,
    wall_normal,
    mode_shape,
):
    block, columns = (3, CX, CY, CZ), pltpu.VMEM((3, GY, CZ), jnp.float32)
    grown = pltpu.VMEM((3, GX, GY, CZ), jnp.float32)
    p0, cs, stiffness, z_low, z_high = call(
        column_kernel,
        (block, block, (CX, CY, CZ), (56, CZ), (56, CZ)),
        (stiffness_table, adjoint_start, sensitivity_source, stiffness_class),
        "hhhh",
        scratch=(
            pltpu.SMEM((8,), jnp.float32),
            pltpu.VMEM(block, jnp.float32),
            pltpu.VMEM(block, jnp.float32),
            pltpu.VMEM((CX, CY, CZ), jnp.int32),
            columns,
            pltpu.SemaphoreType.DMA((3, CX // STEP_X)),
            pltpu.SemaphoreType.DMA,
        ),
    )
    z_next = from_next(z_low, "chord")
    inner, y_low, y_high, x_out = call(
        sweep_kernel,
        (block, (3, GX, 8, CZ), (3, GX, 8, CZ), (3, 6, CY, CZ)),
        (p0, cs),
        "vv",
        scratch=(grown,) * 5,
        flops=1 << 25,
    )
    z_high, y_low = lax.optimization_barrier((z_high, y_low))
    z_prev = from_previous(z_high, "chord")
    cells, owners = wall_cell.reshape(1, WALL), patch_owner.reshape(1, WALL)
    planes, patches = call(
        mark_kernel,
        ((256, WALL), (WALL, PATCH_DEV)),
        (cells, owners, y_low),
        "vvv",
        flops=1 << 25,
        kind=jnp.bfloat16,
    )
    y_low, planes, patches = lax.optimization_barrier((y_low, planes, patches))
    slab = (3, 3, GX, CZ)
    low, high = call(
        pitch_kernel, (slab, slab), (y_low, y_high, z_next, z_prev), "vvvv", scratch=(columns,)
    )
    y_next, y_prev = from_next(low, "pitch"), from_previous(high, "pitch")
    slab = (3, 3, CY, CZ)
    low, high = call(
        span_kernel, (slab, slab), (x_out, z_next, z_prev, y_next, y_prev), "vvvvv", scratch=(columns,)
    )
    x_next, x_prev = from_next(low, "span"), from_previous(high, "span")
    given = (z_next, z_prev, y_next, y_prev)
    work = (
        columns,
        pltpu.VMEM((3, CX // 2, CY, CZ), jnp.float32),
        pltpu.VMEM((3, CX // 2 * CY, CZ), jnp.float32),
        pltpu.VMEM((6 * CZ, CX // 2 * CY), jnp.bfloat16),
    )
    adjoint, share = call(
        middle_kernel,
        (block, (1, WALL)),
        (inner, stiffness, *given, cells, wall_normal),
        "vvvvvvvv",
        scratch=(*work, pltpu.SemaphoreType.DMA),
        out_spaces="hv",
        flops=1 << 30,
    )
    adjoint, sums = call(
        wall_kernel,
        (block, (CHORD * MODES, PATCH_DEV)),
        (
            adjoint, inner, stiffness, *given, x_next, x_prev, share,
            cells, owners, wall_normal, mode_shape, planes, patches,
        ),
        "hvvvvvvvvvvvvvvv",
        scratch=(*work, pltpu.SemaphoreType.DMA((2,))),
        out_spaces="hv",
        aliases={0: 0},
        flops=1 << 30,
    )
    sums = sums.reshape(CHORD, MODES, PATCH_DEV)
    arrived = lax.all_to_all(sums, "chord", split_axis=0, concat_axis=0, tiled=True)
    return adjoint, arrived.sum(axis=0)


def solution(mesh):
    in_specs = (
        P(None, "span", "pitch", "chord"),
        P(None, "span", "pitch", "chord"),
        P("span", "pitch", "chord"),
        P(),
        P(("span", "pitch", "chord")),
        P(("span", "pitch", "chord"), None),
        P(None, ("span", "pitch", "chord")),
        P(None, ("span", "pitch", "chord")),
    )
    out_specs = (P(None, "span", "pitch", "chord"), P(None, ("span", "pitch", "chord")))
    return jax.shard_map(body, mesh=mesh, in_specs=in_specs, out_specs=out_specs, check_vma=False)
```

```python
import functools

import jax
import jax.numpy as jnp
from jax import lax
from jax.experimental import pallas as pl
from jax.experimental.pallas import tpu as pltpu
from jax.sharding import PartitionSpec as P

CX, CY, CZ = 16, 32, 128
PATCH_DEV = 128
MODES = 8
CHORD = 16
WALL = 4096

MASS_SHIFT = 0.5
RELAXATION = 0.8
DIAGONAL_SUM = 10.5
LAME_WEIGHTS = ((3.0, 1.0, 1.0), (1.0, 3.0, 1.0), (1.0, 1.0, 3.0))

STEP = RELAXATION / DIAGONAL_SUM
OWN = 1.0 - STEP * (MASS_SHIFT + 2.0 * sum(LAME_WEIGHTS[0]))
PULL = tuple(tuple(STEP * weight for weight in row) for row in LAME_WEIGHTS)

GX, GY = 24, 48
FIRST, MIDDLE, LAST = 6, 24, 42
HALF = MIDDLE - FIRST
ROWS = 2048
STEP_X = 4

VMEM = pl.BlockSpec(memory_space=pltpu.VMEM)
SMEM = pl.BlockSpec(memory_space=pltpu.SMEM)
HBM = pl.BlockSpec(memory_space=pltpu.HBM)


def iota(shape, dim):
    return lax.broadcasted_iota(jnp.int32, shape, dim)


def shifted_lanes(v):
    lane = iota(v.shape, v.ndim - 1)
    before = jnp.where(lane == 0, 0.0, pltpu.roll(v, 1, v.ndim - 1))
    after = jnp.where(lane == CZ - 1, 0.0, pltpu.roll(v, CZ - 1, v.ndim - 1))
    return before + after


def pick(table, classes):
    low, mid, high = (classes & 1) == 1, (classes & 2) == 2, (classes & 4) == 4
    pairs = [jnp.where(low, table[2 * i + 1], table[2 * i]) for i in range(4)]
    return jnp.where(high, jnp.where(mid, pairs[3], pairs[2]), jnp.where(mid, pairs[1], pairs[0]))


def open_sides():
    sides = []
    for axis in ("span", "pitch", "chord"):
        position, size = lax.axis_index(axis), lax.axis_size(axis)
        sides.append(jnp.where(position > 0, 1.0, 0.0).astype(jnp.float32))
        sides.append(jnp.where(position < size - 1, 1.0, 0.0).astype(jnp.float32))
    return sides


def slots(shape):
    lane = iota(shape, len(shape) - 1)
    plane = (lane * 43) >> 8
    return plane, lane - 6 * plane


def column_kernel(
    table_in, start, source, classes, p0, cs, stiffness, z_low, z_high,
    table, y_in, s_in, c_in, beyond, sems, table_sem,
):
    table_copy = pltpu.make_async_copy(table_in, table, table_sem)
    table_copy.start()
    copies = []
    for g in range(CX // STEP_X):
        part = pl.ds(g * STEP_X, STEP_X)
        copies.append(
            [
                pltpu.make_async_copy(classes.at[part], c_in.at[part], sems.at[0, g]),
                pltpu.make_async_copy(start.at[:, part], y_in.at[:, part], sems.at[1, g]),
                pltpu.make_async_copy(source.at[:, part], s_in.at[:, part], sems.at[2, g]),
            ]
        )
        for copy in copies[-1]:
            copy.start()
    x_lo, x_hi, y_lo, y_hi, z_lo, z_hi = open_sides()

    lane = iota((CY, CZ), 1)
    edge = (lane < 3) | (lane >= CZ - 3)
    values = [jnp.zeros((CY, CZ), jnp.float32) for _ in range(3)]
    pushes = [jnp.zeros((CY, CZ), jnp.float32) for _ in range(3)]
    table_copy.wait()
    for x in range(CX):
        if x % STEP_X == 0:
            for copy in copies[x // STEP_X]:
                copy.wait()
        k = pick(table, c_in[x])
        stiffness[x] = k
        shift = (6 * (x + 2) + 3) % CZ
        for c in range(3):
            value = k * y_in[c, x]
            push = STEP * s_in[c, x]
            p0[c, x] = value
            cs[c, x] = push
            values[c] = values[c] + pltpu.roll(jnp.where(edge, value, 0.0), shift, 1)
            pushes[c] = pushes[c] + pltpu.roll(jnp.where(edge, push, 0.0), shift, 1)

    shape = (GY, CZ)
    plane, slot = slots(shape)
    row = iota(shape, 0)
    keep = jnp.where(row < 8, y_lo, jnp.where(row >= 8 + CY, y_hi, 1.0))
    side = jnp.where(plane < 2, x_lo, jnp.where(plane >= 2 + CX, x_hi, 1.0))
    side = jnp.where(plane < 20, side, 0.0) * keep
    at_high, at_low = slot == 2, slot == 3
    gate = jnp.where(at_high, z_hi, jnp.where(at_low, z_lo, 0.0))
    no_before, no_after = (slot == 0) | (slot == 3), (slot == 2) | (slot == 5)
    pad = jnp.zeros((8, CZ), jnp.float32)
    _, packed_slot = slots((HALF, CZ))

    for c in range(3):
        along = PULL[c][2]

        def flat(v):
            planes = pltpu.roll(v, 6, 1) + pltpu.roll(v, CZ - 6, 1)
            lines = pltpu.roll(v, 1, 0) + pltpu.roll(v, GY - 1, 0)
            return (OWN * v + PULL[c][0] * planes + PULL[c][1] * lines) * side

        def beside(v):
            before = jnp.where(no_before, 0.0, pltpu.roll(v, 1, 1))
            after = jnp.where(no_after, 0.0, pltpu.roll(v, CZ - 1, 1))
            return along * (before + after)

        v0 = jnp.concatenate([pad, values[c], pad], axis=0)
        push = jnp.concatenate([pad, pushes[c], pad], axis=0)
        t1 = flat(v0)
        v1 = t1 + beside(v0) + push
        t2 = flat(v1)
        v2 = t2 + beside(v1) + push + (along * along) * gate * v0
        out1 = along * gate * (flat(t1) + t2 + v2 + (along * along) * v0)
        out2 = (along * along) * gate * (2.0 * t1 + v1)
        out3 = (along * along * along) * gate * v0
        given = jnp.zeros(shape, jnp.float32)
        for far, out in ((1, out1), (2, out2), (3, out3)):
            given = given + pltpu.roll(jnp.where(at_low, out, 0.0), CZ - far, 1)
            given = given + pltpu.roll(jnp.where(at_high, out, 0.0), far, 1)
        beyond[c] = given
        top, rest = beyond[c, FIRST:MIDDLE, :], beyond[c, MIDDLE:LAST, :]
        rows = slice(HALF * c, HALF * (c + 1))
        z_low[rows, :] = jnp.where(packed_slot < 3, top, pltpu.roll(rest, 3, 1))
        z_high[rows, :] = jnp.where(packed_slot >= 3, rest, pltpu.roll(top, CZ - 3, 1))
    for out in (z_low, z_high):
        out[3 * HALF : 56, :] = jnp.zeros((56 - 3 * HALF, CZ), jnp.float32)


def sweep_kernel(p0_in, cs_in, inner, y_low, y_high, x_out, p0, p1, p2, q, cs):
    x_lo, x_hi, y_lo, y_hi, z_lo, z_hi = open_sides()
    shape = (GY, CZ)
    row, lane = iota(shape, 0), iota(shape, 1)
    keep = jnp.where(row < 8, y_lo, jnp.where(row >= 8 + CY, y_hi, 1.0))
    gate = jnp.where(lane == 0, z_lo, jnp.where(lane == CZ - 1, z_hi, 0.0))
    zeros = jnp.zeros(shape, jnp.float32)

    def clear(ref, planes):
        for c in range(3):
            for x in planes:
                ref[c, x] = zeros

    clear(p0, (2, 3, 20, 21))
    clear(p1, (1, 2, 21, 22))
    clear(p2, (0, 1, 22, 23))
    clear(q, (1, 2, 21, 22))
    clear(cs, (1, 2, 3, 20, 21, 22))
    pad = jnp.zeros((8, CZ), jnp.float32)
    for x in range(CX):
        for c in range(3):
            for ref, given in ((p0, p0_in), (cs, cs_in)):
                ref[c, x + 4, 0:8, :] = pad
                ref[c, x + 4, 8 : 8 + CY, :] = given[c, x]
                ref[c, x + 4, 8 + CY : GY, :] = pad

    def across(ref, c, x):
        here = ref[c, x]
        planes = ref[c, x - 1] + ref[c, x + 1]
        lines = pltpu.roll(here, 1, 0) + pltpu.roll(here, GY - 1, 0)
        side = jnp.where(x < 4, x_lo, jnp.where(x >= 4 + CX, x_hi, 1.0))
        return here, (OWN * here + PULL[c][0] * planes + PULL[c][1] * lines) * (keep * side)

    def first(x, carry):
        for c in range(3):
            here, flat = across(p0, c, x)
            new = flat + PULL[c][2] * shifted_lanes(here) + cs[c, x]
            p1[c, x] = new
            q[c, x] = flat + new
        return carry

    lax.fori_loop(3, 21, first, 0, unroll=True)

    def second(x, carry):
        for c in range(3):
            here, flat = across(p1, c, x)
            new = flat + PULL[c][2] * shifted_lanes(here) + cs[c, x]
            p2[c, x] = new + (PULL[c][2] * PULL[c][2] * gate) * p0[c, x]
        return carry

    lax.fori_loop(2, 22, second, 0, unroll=True)

    def third(x):
        values = []
        for c in range(3):
            here, flat = across(p2, c, x)
            new = flat + PULL[c][2] * shifted_lanes(here) + cs[c, x]
            new = new + (PULL[c][2] * PULL[c][2] * gate) * q[c, x]
            y_low[c, x] = new[0:8, :]
            y_high[c, x] = new[8 + CY : GY, :]
            values.append(new[8 : 8 + CY, :])
        return values

    for i, x in enumerate((1, 2, 3, 20, 21, 22)):
        for c, value in enumerate(third(x)):
            x_out[c, i] = value

    def middle(x, carry):
        for c, value in enumerate(third(x)):
            inner[c, x - 4] = value
        return carry

    lax.fori_loop(4, 20, middle, 0, unroll=True)


def unpack(z_prev, z_next, columns):
    _, slot = slots((HALF, CZ))
    for c in range(3):
        rows = slice(HALF * c, HALF * (c + 1))
        above, below = z_next[rows, :], z_prev[rows, :]
        columns[c, 0:8, :] = jnp.zeros((8, CZ), jnp.float32)
        columns[c, GY - 8 : GY, :] = jnp.zeros((8, CZ), jnp.float32)
        columns[c, FIRST:MIDDLE, :] = jnp.where(slot < 3, above, pltpu.roll(below, 3, 1))
        columns[c, MIDDLE:LAST, :] = jnp.where(slot < 3, pltpu.roll(above, CZ - 3, 1), below)


def chord_part(columns, c, x, start, size):
    lane = iota((size, CZ), 1)
    placed = pltpu.roll(columns[c, start : start + size, :], (CZ - 3 - 6 * (x - 2)) % CZ, 1)
    return jnp.where((lane < 3) | (lane >= CZ - 3), placed, 0.0)


def pitch_kernel(y_low, y_high, z_prev, z_next, low, high, columns):
    unpack(z_prev, z_next, columns)
    for c in range(3):
        for x in range(1, 23):
            for tile, out, start, first in ((y_low, low, 0, 5), (y_high, high, 40, 0)):
                value = tile[c, x]
                if 2 <= x < 22:
                    value = value + chord_part(columns, c, x, start, 8)
                for j in range(3):
                    out[c, j, x : x + 1, :] = value[first + j : first + j + 1, :]


def pitch_rows(y_next, y_prev, c, x):
    row = iota((8, CZ), 0)
    bottom = jnp.zeros((8, CZ), jnp.float32)
    top = jnp.zeros((8, CZ), jnp.float32)
    for j in range(3):
        bottom = jnp.where(row == j, y_prev[c, j, x : x + 1, :], bottom)
        top = jnp.where(row == 5 + j, y_next[c, j, x : x + 1, :], top)
    return bottom, top


def span_kernel(x_out, z_prev, z_next, y_next, y_prev, low, high, columns):
    unpack(z_prev, z_next, columns)
    for c in range(3):
        for i, x in enumerate((1, 2, 3, 20, 21, 22)):
            out, j = (low, i) if i < 3 else (high, i - 3)
            value = x_out[c, i]
            if 2 <= x < 22:
                value = value + chord_part(columns, c, x, 8, CY)
            out[c, j] = value
            bottom, top = pitch_rows(y_next, y_prev, c, x)
            out[c, j, 0:8, :] += bottom
            out[c, j, 24:32, :] += top


def finish_planes(planes, inner, z_prev, z_next, y_next, y_prev, stiffness, columns, values, part, field, span):
    unpack(z_prev, z_next, columns)
    zeros = jnp.zeros((8, CZ), jnp.float32)
    for i, x in enumerate(planes):
        ratio = 1.0 / stiffness[x]
        for c in range(3):
            value = inner[c, x] + chord_part(columns, c, x + 4, 8, CY)
            bottom, top = pitch_rows(y_next, y_prev, c, x + 4)
            value = value + jnp.concatenate([bottom, zeros, zeros, top], axis=0)
            value = span(value, c, x)
            values[c, i] = value * ratio
            part[c, CY * i : CY * (i + 1), :] = value
    for c in range(3):
        for g in range(CY * len(planes) // 128):
            block = part[c, 128 * g : 128 * (g + 1), :].T
            first = block.astype(jnp.bfloat16)
            second = (block - first.astype(jnp.float32)).astype(jnp.bfloat16)
            field[256 * c : 256 * c + 128, 128 * g : 128 * (g + 1)] = first
            field[256 * c + 128 : 256 * c + 256, 128 * g : 128 * (g + 1)] = second


def marks(length, place):
    return (iota((length, place.shape[1]), 0) == place).astype(jnp.bfloat16)


def mark_kernel(wall_cell, patch_owner, after, planes, patches):
    for step in range(WALL // 512):
        here = slice(step * 512, (step + 1) * 512)
        plane = wall_cell[:, here] >> 7
        place = jnp.where(plane < 128, plane, jnp.where(plane >= 384, plane - 256, -1))
        planes[:, here] = marks(256, place)
        patches[here, :] = marks(PATCH_DEV, patch_owner[:, here] & 127).T


def normal_share(field, planes, cell, normals):
    count = cell.shape[1]
    picked = jnp.dot(field[...], planes, preferred_element_type=jnp.float32)
    value = jnp.zeros((CZ, count), jnp.float32)
    for c in range(3):
        part = picked[256 * c : 256 * c + 128] + picked[256 * c + 128 : 256 * c + 256]
        value = value + normals[c : c + 1] * part
    value = jnp.where(iota((CZ, count), 0) == (cell & 127), value, 0.0)
    return jnp.sum(value, axis=0, keepdims=True)


def middle_kernel(
    inner, stiffness, z_prev, z_next, y_next, y_prev, wall_cell, wall_normal,
    adjoint, share, columns, values, part, field, sem,
):
    def as_is(value, c, x):
        return value

    finish_planes(
        range(4, 12), inner, z_prev, z_next, y_next, y_prev,
        stiffness, columns, values, part, field, as_is,
    )
    copy = pltpu.make_async_copy(values, adjoint.at[:, 4:12], sem)
    copy.start()
    for step in range(WALL // ROWS):
        here = slice(step * ROWS, (step + 1) * ROWS)
        cell = wall_cell[:, here]
        share[:, here] = normal_share(
            field, marks(256, (cell >> 7) - 128), cell, wall_normal[:, here]
        )
    copy.wait()


def wall_kernel(
    given, inner, stiffness, z_prev, z_next, y_next, y_prev, x_next, x_prev, share,
    wall_cell, patch_owner, wall_normal, mode_shape, planes, patches,
    adjoint, sums, columns, values, part, field, sems,
):
    def span(value, c, x):
        if x < 3:
            return value + x_prev[c, x]
        if x >= CX - 3:
            return value + x_next[c, x - (CX - 3)]
        return value

    finish_planes(
        (0, 1, 2, 3, 12, 13, 14, 15), inner, z_prev, z_next, y_next, y_prev,
        stiffness, columns, values, part, field, span,
    )
    copies = [
        pltpu.make_async_copy(values.at[:, 0:4], adjoint.at[:, 0:4], sems.at[0]),
        pltpu.make_async_copy(values.at[:, 4:8], adjoint.at[:, 12:16], sems.at[1]),
    ]
    for copy in copies:
        copy.start()
    height = CHORD * MODES
    total = jnp.zeros((2 * height, PATCH_DEV), jnp.float32)
    for step in range(WALL // ROWS):
        here = slice(step * ROWS, (step + 1) * ROWS)
        cell, owner = wall_cell[:, here], patch_owner[:, here]
        normal = share[:, here] + normal_share(field, planes[:, here], cell, wall_normal[:, here])
        parts = mode_shape[:, here] * normal
        device = owner >> 7
        spread = jnp.concatenate([jnp.where(device == o, parts, 0.0) for o in range(CHORD)], axis=0)
        first = spread.astype(jnp.bfloat16)
        second = (spread - first.astype(jnp.float32)).astype(jnp.bfloat16)
        both = jnp.concatenate([first, second], axis=0)
        total = total + jnp.dot(both, patches[here, :], preferred_element_type=jnp.float32)
    sums[...] = total[0:height] + total[height : 2 * height]
    for copy in copies:
        copy.wait()


def call(
    kernel, outs, operands, spaces, scratch=(), out_spaces=None, aliases=None, flops=0, kind=jnp.float32
):
    spec = {"h": HBM, "s": SMEM, "v": VMEM}
    shapes = tuple(jax.ShapeDtypeStruct(shape, kind) for shape in outs)
    moved = sum(4 * o.size for o in operands) + sum(4 * s.size for s in shapes)
    operands = [
        pltpu.with_memory_space_constraint(o, pltpu.HBM) if space == "h" else o
        for o, space in zip(operands, spaces)
    ]
    return pl.pallas_call(
        kernel,
        out_shape=shapes,
        in_specs=[spec[space] for space in spaces],
        out_specs=tuple(spec[space] for space in out_spaces or "v" * len(outs)),
        scratch_shapes=list(scratch),
        input_output_aliases=aliases or {},
        cost_estimate=pl.CostEstimate(flops=flops, bytes_accessed=moved, transcendentals=0),
        compiler_params=pltpu.CompilerParams(vmem_limit_bytes=40 << 20),
    )(*operands)


def pairs(axis):
    return [(i, i + 1) for i in range(lax.axis_size(axis) - 1)]


def from_next(low, axis):
    return lax.ppermute(low, axis, [(j, i) for i, j in pairs(axis)])


def from_previous(high, axis):
    return lax.ppermute(high, axis, pairs(axis))


def body(
    adjoint_start,
    sensitivity_source,
    stiffness_class,
    stiffness_table,
    wall_cell,
    patch_owner,
    wall_normal,
    mode_shape,
):
    block, columns = (3, CX, CY, CZ), pltpu.VMEM((3, GY, CZ), jnp.float32)
    grown = pltpu.VMEM((3, GX, GY, CZ), jnp.float32)
    p0, cs, stiffness, z_low, z_high = call(
        column_kernel,
        (block, block, (CX, CY, CZ), (56, CZ), (56, CZ)),
        (stiffness_table, adjoint_start, sensitivity_source, stiffness_class),
        "hhhh",
        scratch=(
            pltpu.SMEM((8,), jnp.float32),
            pltpu.VMEM(block, jnp.float32),
            pltpu.VMEM(block, jnp.float32),
            pltpu.VMEM((CX, CY, CZ), jnp.int32),
            columns,
            pltpu.SemaphoreType.DMA((3, CX // STEP_X)),
            pltpu.SemaphoreType.DMA,
        ),
    )
    z_prev, z_next = from_previous(z_high, "chord"), from_next(z_low, "chord")
    inner, y_low, y_high, x_out = call(
        sweep_kernel,
        (block, (3, GX, 8, CZ), (3, GX, 8, CZ), (3, 6, CY, CZ)),
        (p0, cs),
        "vv",
        scratch=(grown,) * 5,
        flops=1 << 25,
    )
    cells, owners = wall_cell.reshape(1, WALL), patch_owner.reshape(1, WALL)
    planes, patches = call(
        mark_kernel,
        ((256, WALL), (WALL, PATCH_DEV)),
        (cells, owners, y_low),
        "vvv",
        flops=1 << 25,
        kind=jnp.bfloat16,
    )
    y_low, planes, patches = lax.optimization_barrier((y_low, planes, patches))
    slab = (3, 3, GX, CZ)
    low, high = call(
        pitch_kernel, (slab, slab), (y_low, y_high, z_prev, z_next), "vvvv", scratch=(columns,)
    )
    y_next, y_prev = from_next(low, "pitch"), from_previous(high, "pitch")
    slab = (3, 3, CY, CZ)
    low, high = call(
        span_kernel, (slab, slab), (x_out, z_prev, z_next, y_next, y_prev), "vvvvv", scratch=(columns,)
    )
    x_next, x_prev = from_next(low, "span"), from_previous(high, "span")
    given = (z_prev, z_next, y_next, y_prev)
    work = (
        columns,
        pltpu.VMEM((3, CX // 2, CY, CZ), jnp.float32),
        pltpu.VMEM((3, CX // 2 * CY, CZ), jnp.float32),
        pltpu.VMEM((6 * CZ, CX // 2 * CY), jnp.bfloat16),
    )
    adjoint, share = call(
        middle_kernel,
        (block, (1, WALL)),
        (inner, stiffness, *given, cells, wall_normal),
        "vvvvvvvv",
        scratch=(*work, pltpu.SemaphoreType.DMA),
        out_spaces="hv",
        flops=1 << 30,
    )
    adjoint, sums = call(
        wall_kernel,
        (block, (CHORD * MODES, PATCH_DEV)),
        (
            adjoint, inner, stiffness, *given, x_next, x_prev, share,
            cells, owners, wall_normal, mode_shape, planes, patches,
        ),
        "hvvvvvvvvvvvvvvv",
        scratch=(*work, pltpu.SemaphoreType.DMA((2,))),
        out_spaces="hv",
        aliases={0: 0},
        flops=1 << 30,
    )
    sums = sums.reshape(CHORD, MODES, PATCH_DEV)
    arrived = lax.all_to_all(sums, "chord", split_axis=0, concat_axis=0, tiled=True)
    return adjoint, arrived.sum(axis=0)


def solution(mesh):
    in_specs = (
        P(None, "span", "pitch", "chord"),
        P(None, "span", "pitch", "chord"),
        P("span", "pitch", "chord"),
        P(),
        P(("span", "pitch", "chord")),
        P(("span", "pitch", "chord"), None),
        P(None, ("span", "pitch", "chord")),
        P(None, ("span", "pitch", "chord")),
    )
    out_specs = (P(None, "span", "pitch", "chord"), P(None, ("span", "pitch", "chord")))
    return jax.shard_map(body, mesh=mesh, in_specs=in_specs, out_specs=out_specs, check_vma=False)
```

```python
import functools

import jax
import jax.numpy as jnp
from jax import lax
from jax.experimental import pallas as pl
from jax.experimental.pallas import tpu as pltpu
from jax.sharding import PartitionSpec as P

CX, CY, CZ = 16, 32, 128
PATCH_DEV = 128
MODES = 8
CHORD = 16
WALL = 4096

MASS_SHIFT = 0.5
RELAXATION = 0.8
DIAGONAL_SUM = 10.5
LAME_WEIGHTS = ((3.0, 1.0, 1.0), (1.0, 3.0, 1.0), (1.0, 1.0, 3.0))

STEP = RELAXATION / DIAGONAL_SUM
OWN = 1.0 - STEP * (MASS_SHIFT + 2.0 * sum(LAME_WEIGHTS[0]))
PULL = tuple(tuple(STEP * weight for weight in row) for row in LAME_WEIGHTS)

GX, GY = 24, 48
FIRST, MIDDLE, LAST = 6, 24, 42
HALF = MIDDLE - FIRST
ROWS = 2048
STEP_X = 4

VMEM = pl.BlockSpec(memory_space=pltpu.VMEM)
SMEM = pl.BlockSpec(memory_space=pltpu.SMEM)
HBM = pl.BlockSpec(memory_space=pltpu.HBM)


def iota(shape, dim):
    return lax.broadcasted_iota(jnp.int32, shape, dim)


def shifted_lanes(v):
    lane = iota(v.shape, v.ndim - 1)
    before = jnp.where(lane == 0, 0.0, pltpu.roll(v, 1, v.ndim - 1))
    after = jnp.where(lane == CZ - 1, 0.0, pltpu.roll(v, CZ - 1, v.ndim - 1))
    return before + after


def pick(table, classes):
    low, mid, high = (classes & 1) == 1, (classes & 2) == 2, (classes & 4) == 4
    pairs = [jnp.where(low, table[2 * i + 1], table[2 * i]) for i in range(4)]
    return jnp.where(high, jnp.where(mid, pairs[3], pairs[2]), jnp.where(mid, pairs[1], pairs[0]))


def open_sides():
    sides = []
    for axis in ("span", "pitch", "chord"):
        position, size = lax.axis_index(axis), lax.axis_size(axis)
        sides.append(jnp.where(position > 0, 1.0, 0.0).astype(jnp.float32))
        sides.append(jnp.where(position < size - 1, 1.0, 0.0).astype(jnp.float32))
    return sides


def slots(shape):
    lane = iota(shape, len(shape) - 1)
    plane = (lane * 43) >> 8
    return plane, lane - 6 * plane


def column_kernel(
    table_in, start, source, classes, p0, cs, stiffness, z_low, z_high,
    table, y_in, s_in, c_in, beyond, sems, table_sem,
):
    table_copy = pltpu.make_async_copy(table_in, table, table_sem)
    table_copy.start()
    copies = []
    for g in range(CX // STEP_X):
        part = pl.ds(g * STEP_X, STEP_X)
        copies.append(
            [
                pltpu.make_async_copy(classes.at[part], c_in.at[part], sems.at[0, g]),
                pltpu.make_async_copy(start.at[:, part], y_in.at[:, part], sems.at[1, g]),
                pltpu.make_async_copy(source.at[:, part], s_in.at[:, part], sems.at[2, g]),
            ]
        )
        for copy in copies[-1]:
            copy.start()
    x_lo, x_hi, y_lo, y_hi, z_lo, z_hi = open_sides()

    lane = iota((CY, CZ), 1)
    edge = (lane < 3) | (lane >= CZ - 3)
    values = [jnp.zeros((CY, CZ), jnp.float32) for _ in range(3)]
    pushes = [jnp.zeros((CY, CZ), jnp.float32) for _ in range(3)]
    table_copy.wait()
    for x in range(CX):
        if x % STEP_X == 0:
            for copy in copies[x // STEP_X]:
                copy.wait()
        k = pick(table, c_in[x])
        stiffness[x] = k
        shift = (6 * (x + 2) + 3) % CZ
        for c in range(3):
            value = k * y_in[c, x]
            push = STEP * s_in[c, x]
            p0[c, x] = value
            cs[c, x] = push
            values[c] = values[c] + pltpu.roll(jnp.where(edge, value, 0.0), shift, 1)
            pushes[c] = pushes[c] + pltpu.roll(jnp.where(edge, push, 0.0), shift, 1)

    shape = (GY, CZ)
    plane, slot = slots(shape)
    row = iota(shape, 0)
    keep = jnp.where(row < 8, y_lo, jnp.where(row >= 8 + CY, y_hi, 1.0))
    side = jnp.where(plane < 2, x_lo, jnp.where(plane >= 2 + CX, x_hi, 1.0))
    side = jnp.where(plane < 20, side, 0.0) * keep
    at_high, at_low = slot == 2, slot == 3
    gate = jnp.where(at_high, z_hi, jnp.where(at_low, z_lo, 0.0))
    no_before, no_after = (slot == 0) | (slot == 3), (slot == 2) | (slot == 5)
    pad = jnp.zeros((8, CZ), jnp.float32)
    _, packed_slot = slots((HALF, CZ))

    for c in range(3):
        along = PULL[c][2]

        def flat(v):
            planes = pltpu.roll(v, 6, 1) + pltpu.roll(v, CZ - 6, 1)
            lines = pltpu.roll(v, 1, 0) + pltpu.roll(v, GY - 1, 0)
            return (OWN * v + PULL[c][0] * planes + PULL[c][1] * lines) * side

        def beside(v):
            before = jnp.where(no_before, 0.0, pltpu.roll(v, 1, 1))
            after = jnp.where(no_after, 0.0, pltpu.roll(v, CZ - 1, 1))
            return along * (before + after)

        v0 = jnp.concatenate([pad, values[c], pad], axis=0)
        push = jnp.concatenate([pad, pushes[c], pad], axis=0)
        t1 = flat(v0)
        v1 = t1 + beside(v0) + push
        t2 = flat(v1)
        v2 = t2 + beside(v1) + push + (along * along) * gate * v0
        out1 = along * gate * (flat(t1) + t2 + v2 + (along * along) * v0)
        out2 = (along * along) * gate * (2.0 * t1 + v1)
        out3 = (along * along * along) * gate * v0
        given = jnp.zeros(shape, jnp.float32)
        for far, out in ((1, out1), (2, out2), (3, out3)):
            given = given + pltpu.roll(jnp.where(at_low, out, 0.0), CZ - far, 1)
            given = given + pltpu.roll(jnp.where(at_high, out, 0.0), far, 1)
        beyond[c] = given
        top, rest = beyond[c, FIRST:MIDDLE, :], beyond[c, MIDDLE:LAST, :]
        rows = slice(HALF * c, HALF * (c + 1))
        z_low[rows, :] = jnp.where(packed_slot < 3, top, pltpu.roll(rest, 3, 1))
        z_high[rows, :] = jnp.where(packed_slot >= 3, rest, pltpu.roll(top, CZ - 3, 1))
    for out in (z_low, z_high):
        out[3 * HALF : 56, :] = jnp.zeros((56 - 3 * HALF, CZ), jnp.float32)


def sweep_kernel(p0_in, cs_in, inner, y_low, y_high, x_out, p0, p1, p2, q, cs):
    x_lo, x_hi, y_lo, y_hi, z_lo, z_hi = open_sides()
    shape = (GY, CZ)
    row, lane = iota(shape, 0), iota(shape, 1)
    keep = jnp.where(row < 8, y_lo, jnp.where(row >= 8 + CY, y_hi, 1.0))
    gate = jnp.where(lane == 0, z_lo, jnp.where(lane == CZ - 1, z_hi, 0.0))
    zeros = jnp.zeros(shape, jnp.float32)

    def clear(ref, planes):
        for c in range(3):
            for x in planes:
                ref[c, x] = zeros

    clear(p0, (2, 3, 20, 21))
    clear(p1, (1, 2, 21, 22))
    clear(p2, (0, 1, 22, 23))
    clear(q, (1, 2, 21, 22))
    clear(cs, (1, 2, 3, 20, 21, 22))
    pad = jnp.zeros((8, CZ), jnp.float32)
    for x in range(CX):
        for c in range(3):
            for ref, given in ((p0, p0_in), (cs, cs_in)):
                ref[c, x + 4, 0:8, :] = pad
                ref[c, x + 4, 8 : 8 + CY, :] = given[c, x]
                ref[c, x + 4, 8 + CY : GY, :] = pad

    def across(ref, c, x):
        here = ref[c, x]
        planes = ref[c, x - 1] + ref[c, x + 1]
        lines = pltpu.roll(here, 1, 0) + pltpu.roll(here, GY - 1, 0)
        side = jnp.where(x < 4, x_lo, jnp.where(x >= 4 + CX, x_hi, 1.0))
        return here, (OWN * here + PULL[c][0] * planes + PULL[c][1] * lines) * (keep * side)

    def first(x, carry):
        for c in range(3):
            here, flat = across(p0, c, x)
            new = flat + PULL[c][2] * shifted_lanes(here) + cs[c, x]
            p1[c, x] = new
            q[c, x] = flat + new
        return carry

    lax.fori_loop(3, 21, first, 0, unroll=True)

    def second(x, carry):
        for c in range(3):
            here, flat = across(p1, c, x)
            new = flat + PULL[c][2] * shifted_lanes(here) + cs[c, x]
            p2[c, x] = new + (PULL[c][2] * PULL[c][2] * gate) * p0[c, x]
        return carry

    lax.fori_loop(2, 22, second, 0, unroll=True)

    def third(x):
        values = []
        for c in range(3):
            here, flat = across(p2, c, x)
            new = flat + PULL[c][2] * shifted_lanes(here) + cs[c, x]
            new = new + (PULL[c][2] * PULL[c][2] * gate) * q[c, x]
            y_low[c, x] = new[0:8, :]
            y_high[c, x] = new[8 + CY : GY, :]
            values.append(new[8 : 8 + CY, :])
        return values

    for i, x in enumerate((1, 2, 3, 20, 21, 22)):
        for c, value in enumerate(third(x)):
            x_out[c, i] = value

    def middle(x, carry):
        for c, value in enumerate(third(x)):
            inner[c, x - 4] = value
        return carry

    lax.fori_loop(4, 20, middle, 0, unroll=True)


def unpack(z_next, z_prev, columns):
    _, slot = slots((HALF, CZ))
    for c in range(3):
        rows = slice(HALF * c, HALF * (c + 1))
        above, below = z_next[rows, :], z_prev[rows, :]
        columns[c, 0:8, :] = jnp.zeros((8, CZ), jnp.float32)
        columns[c, GY - 8 : GY, :] = jnp.zeros((8, CZ), jnp.float32)
        columns[c, FIRST:MIDDLE, :] = jnp.where(slot < 3, above, pltpu.roll(below, 3, 1))
        columns[c, MIDDLE:LAST, :] = jnp.where(slot < 3, pltpu.roll(above, CZ - 3, 1), below)


def chord_part(columns, c, x, start, size):
    lane = iota((size, CZ), 1)
    placed = pltpu.roll(columns[c, start : start + size, :], (CZ - 3 - 6 * (x - 2)) % CZ, 1)
    return jnp.where((lane < 3) | (lane >= CZ - 3), placed, 0.0)


def pitch_kernel(y_low, y_high, z_next, z_prev, low, high, columns):
    unpack(z_next, z_prev, columns)
    for c in range(3):
        for x in range(1, 23):
            for tile, out, start, first in ((y_low, low, 0, 5), (y_high, high, 40, 0)):
                value = tile[c, x]
                if 2 <= x < 22:
                    value = value + chord_part(columns, c, x, start, 8)
                for j in range(3):
                    out[c, j, x : x + 1, :] = value[first + j : first + j + 1, :]


def pitch_rows(y_next, y_prev, c, x):
    row = iota((8, CZ), 0)
    bottom = jnp.zeros((8, CZ), jnp.float32)
    top = jnp.zeros((8, CZ), jnp.float32)
    for j in range(3):
        bottom = jnp.where(row == j, y_prev[c, j, x : x + 1, :], bottom)
        top = jnp.where(row == 5 + j, y_next[c, j, x : x + 1, :], top)
    return bottom, top


def span_kernel(x_out, z_next, z_prev, y_next, y_prev, low, high, columns):
    unpack(z_next, z_prev, columns)
    for c in range(3):
        for i, x in enumerate((1, 2, 3, 20, 21, 22)):
            out, j = (low, i) if i < 3 else (high, i - 3)
            value = x_out[c, i]
            if 2 <= x < 22:
                value = value + chord_part(columns, c, x, 8, CY)
            out[c, j] = value
            bottom, top = pitch_rows(y_next, y_prev, c, x)
            out[c, j, 0:8, :] += bottom
            out[c, j, 24:32, :] += top


def finish_planes(planes, inner, z_next, z_prev, y_next, y_prev, stiffness, columns, values, part, field, span):
    unpack(z_next, z_prev, columns)
    zeros = jnp.zeros((8, CZ), jnp.float32)
    for i, x in enumerate(planes):
        ratio = 1.0 / stiffness[x]
        for c in range(3):
            value = inner[c, x] + chord_part(columns, c, x + 4, 8, CY)
            bottom, top = pitch_rows(y_next, y_prev, c, x + 4)
            value = value + jnp.concatenate([bottom, zeros, zeros, top], axis=0)
            value = span(value, c, x)
            values[c, i] = value * ratio
            part[c, CY * i : CY * (i + 1), :] = value
    for c in range(3):
        for g in range(CY * len(planes) // 128):
            block = part[c, 128 * g : 128 * (g + 1), :].T
            first = block.astype(jnp.bfloat16)
            second = (block - first.astype(jnp.float32)).astype(jnp.bfloat16)
            field[256 * c : 256 * c + 128, 128 * g : 128 * (g + 1)] = first
            field[256 * c + 128 : 256 * c + 256, 128 * g : 128 * (g + 1)] = second


def marks(length, place):
    return (iota((length, place.shape[1]), 0) == place).astype(jnp.bfloat16)


def mark_kernel(wall_cell, patch_owner, after, planes, patches):
    for step in range(WALL // 512):
        here = slice(step * 512, (step + 1) * 512)
        plane = wall_cell[:, here] >> 7
        place = jnp.where(plane < 128, plane, jnp.where(plane >= 384, plane - 256, -1))
        planes[:, here] = marks(256, place)
        patches[here, :] = marks(PATCH_DEV, patch_owner[:, here] & 127).T


def normal_share(field, planes, cell, normals):
    count = cell.shape[1]
    picked = jnp.dot(field[...], planes, preferred_element_type=jnp.float32)
    value = jnp.zeros((CZ, count), jnp.float32)
    for c in range(3):
        part = picked[256 * c : 256 * c + 128] + picked[256 * c + 128 : 256 * c + 256]
        value = value + normals[c : c + 1] * part
    value = jnp.where(iota((CZ, count), 0) == (cell & 127), value, 0.0)
    return jnp.sum(value, axis=0, keepdims=True)


def middle_kernel(
    inner, stiffness, z_next, z_prev, y_next, y_prev, wall_cell, wall_normal,
    adjoint, share, columns, values, part, field, sem,
):
    def as_is(value, c, x):
        return value

    finish_planes(
        range(4, 12), inner, z_next, z_prev, y_next, y_prev,
        stiffness, columns, values, part, field, as_is,
    )
    copy = pltpu.make_async_copy(values, adjoint.at[:, 4:12], sem)
    copy.start()
    for step in range(WALL // ROWS):
        here = slice(step * ROWS, (step + 1) * ROWS)
        cell = wall_cell[:, here]
        share[:, here] = normal_share(
            field, marks(256, (cell >> 7) - 128), cell, wall_normal[:, here]
        )
    copy.wait()


def wall_kernel(
    given, inner, stiffness, z_next, z_prev, y_next, y_prev, x_next, x_prev, share,
    wall_cell, patch_owner, wall_normal, mode_shape, planes, patches,
    adjoint, sums, columns, values, part, field, sems,
):
    def span(value, c, x):
        if x < 3:
            return value + x_prev[c, x]
        if x >= CX - 3:
            return value + x_next[c, x - (CX - 3)]
        return value

    finish_planes(
        (0, 1, 2, 3, 12, 13, 14, 15), inner, z_next, z_prev, y_next, y_prev,
        stiffness, columns, values, part, field, span,
    )
    copies = [
        pltpu.make_async_copy(values.at[:, 0:4], adjoint.at[:, 0:4], sems.at[0]),
        pltpu.make_async_copy(values.at[:, 4:8], adjoint.at[:, 12:16], sems.at[1]),
    ]
    for copy in copies:
        copy.start()
    total = jnp.zeros((2 * CHORD * MODES, PATCH_DEV), jnp.float32)
    for step in range(WALL // ROWS):
        here = slice(step * ROWS, (step + 1) * ROWS)
        cell, owner = wall_cell[:, here], patch_owner[:, here]
        normal = share[:, here] + normal_share(field, planes[:, here], cell, wall_normal[:, here])
        parts = mode_shape[:, here] * normal
        high = parts.astype(jnp.bfloat16).astype(jnp.float32)
        pieces = jnp.concatenate([high, parts - high], axis=0).astype(jnp.bfloat16)
        device = jnp.broadcast_to((owner >> 7).astype(jnp.float32), pieces.shape).astype(jnp.bfloat16)
        both = jnp.concatenate(
            [jnp.where(device == o, pieces, jnp.bfloat16(0)) for o in range(CHORD)], axis=0
        )
        total = total + jnp.dot(both, patches[here, :], preferred_element_type=jnp.float32)
    for o in range(CHORD):
        first, second = 2 * MODES * o, MODES * (2 * o + 1)
        sums[MODES * o : MODES * (o + 1), :] = total[first : first + MODES] + total[second : second + MODES]
    for copy in copies:
        copy.wait()


def call(
    kernel, outs, operands, spaces, scratch=(), out_spaces=None, aliases=None, flops=0, kind=jnp.float32
):
    spec = {"h": HBM, "s": SMEM, "v": VMEM}
    shapes = tuple(jax.ShapeDtypeStruct(shape, kind) for shape in outs)
    moved = sum(4 * o.size for o in operands) + sum(4 * s.size for s in shapes)
    operands = [
        pltpu.with_memory_space_constraint(o, pltpu.HBM) if space == "h" else o
        for o, space in zip(operands, spaces)
    ]
    return pl.pallas_call(
        kernel,
        out_shape=shapes,
        in_specs=[spec[space] for space in spaces],
        out_specs=tuple(spec[space] for space in out_spaces or "v" * len(outs)),
        scratch_shapes=list(scratch),
        input_output_aliases=aliases or {},
        cost_estimate=pl.CostEstimate(flops=flops, bytes_accessed=moved, transcendentals=0),
        compiler_params=pltpu.CompilerParams(vmem_limit_bytes=40 << 20),
    )(*operands)


def pairs(axis):
    return [(i, i + 1) for i in range(lax.axis_size(axis) - 1)]


def from_next(low, axis):
    return lax.ppermute(low, axis, [(j, i) for i, j in pairs(axis)])


def from_previous(high, axis):
    return lax.ppermute(high, axis, pairs(axis))


def body(
    adjoint_start,
    sensitivity_source,
    stiffness_class,
    stiffness_table,
    wall_cell,
    patch_owner,
    wall_normal,
    mode_shape,
):
    block, columns = (3, CX, CY, CZ), pltpu.VMEM((3, GY, CZ), jnp.float32)
    grown = pltpu.VMEM((3, GX, GY, CZ), jnp.float32)
    p0, cs, stiffness, z_low, z_high = call(
        column_kernel,
        (block, block, (CX, CY, CZ), (56, CZ), (56, CZ)),
        (stiffness_table, adjoint_start, sensitivity_source, stiffness_class),
        "hhhh",
        scratch=(
            pltpu.SMEM((8,), jnp.float32),
            pltpu.VMEM(block, jnp.float32),
            pltpu.VMEM(block, jnp.float32),
            pltpu.VMEM((CX, CY, CZ), jnp.int32),
            columns,
            pltpu.SemaphoreType.DMA((3, CX // STEP_X)),
            pltpu.SemaphoreType.DMA,
        ),
    )
    z_prev, z_next = from_previous(z_high, "chord"), from_next(z_low, "chord")
    inner, y_low, y_high, x_out = call(
        sweep_kernel,
        (block, (3, GX, 8, CZ), (3, GX, 8, CZ), (3, 6, CY, CZ)),
        (p0, cs),
        "vv",
        scratch=(grown,) * 5,
        flops=1 << 25,
    )
    cells, owners = wall_cell.reshape(1, WALL), patch_owner.reshape(1, WALL)
    planes, patches = call(
        mark_kernel,
        ((256, WALL), (WALL, PATCH_DEV)),
        (cells, owners, y_low),
        "vvv",
        flops=1 << 25,
        kind=jnp.bfloat16,
    )
    y_low, planes, patches = lax.optimization_barrier((y_low, planes, patches))
    slab = (3, 3, GX, CZ)
    low, high = call(
        pitch_kernel, (slab, slab), (y_low, y_high, z_next, z_prev), "vvvv", scratch=(columns,)
    )
    y_next, y_prev = from_next(low, "pitch"), from_previous(high, "pitch")
    slab = (3, 3, CY, CZ)
    low, high = call(
        span_kernel, (slab, slab), (x_out, z_next, z_prev, y_next, y_prev), "vvvvv", scratch=(columns,)
    )
    x_next, x_prev = from_next(low, "span"), from_previous(high, "span")
    given = (z_next, z_prev, y_next, y_prev)
    work = (
        columns,
        pltpu.VMEM((3, CX // 2, CY, CZ), jnp.float32),
        pltpu.VMEM((3, CX // 2 * CY, CZ), jnp.float32),
        pltpu.VMEM((6 * CZ, CX // 2 * CY), jnp.bfloat16),
    )
    adjoint, share = call(
        middle_kernel,
        (block, (1, WALL)),
        (inner, stiffness, *given, cells, wall_normal),
        "vvvvvvvv",
        scratch=(*work, pltpu.SemaphoreType.DMA),
        out_spaces="hv",
        flops=1 << 30,
    )
    adjoint, sums = call(
        wall_kernel,
        (block, (CHORD * MODES, PATCH_DEV)),
        (
            adjoint, inner, stiffness, *given, x_next, x_prev, share,
            cells, owners, wall_normal, mode_shape, planes, patches,
        ),
        "hvvvvvvvvvvvvvvv",
        scratch=(*work, pltpu.SemaphoreType.DMA((2,))),
        out_spaces="hv",
        aliases={0: 0},
        flops=1 << 30,
    )
    sums = sums.reshape(CHORD, MODES, PATCH_DEV)
    arrived = lax.all_to_all(sums, "chord", split_axis=0, concat_axis=0, tiled=True)
    return adjoint, arrived.sum(axis=0)


def solution(mesh):
    in_specs = (
        P(None, "span", "pitch", "chord"),
        P(None, "span", "pitch", "chord"),
        P("span", "pitch", "chord"),
        P(),
        P(("span", "pitch", "chord")),
        P(("span", "pitch", "chord"), None),
        P(None, ("span", "pitch", "chord")),
        P(None, ("span", "pitch", "chord")),
    )
    out_specs = (P(None, "span", "pitch", "chord"), P(None, ("span", "pitch", "chord")))
    return jax.shard_map(body, mesh=mesh, in_specs=in_specs, out_specs=out_specs, check_vma=False)
```

```python
import functools

import jax
import jax.numpy as jnp
from jax import lax
from jax.experimental import pallas as pl
from jax.experimental.pallas import tpu as pltpu
from jax.sharding import PartitionSpec as P

CX, CY, CZ = 16, 32, 128
PATCH_DEV = 128
MODES = 8
CHORD = 16
WALL = 4096

MASS_SHIFT = 0.5
RELAXATION = 0.8
DIAGONAL_SUM = 10.5
LAME_WEIGHTS = ((3.0, 1.0, 1.0), (1.0, 3.0, 1.0), (1.0, 1.0, 3.0))

STEP = RELAXATION / DIAGONAL_SUM
OWN = 1.0 - STEP * (MASS_SHIFT + 2.0 * sum(LAME_WEIGHTS[0]))
PULL = tuple(tuple(STEP * weight for weight in row) for row in LAME_WEIGHTS)

GX, GY = 24, 48
FIRST, MIDDLE, LAST = 6, 24, 42
HALF = MIDDLE - FIRST
ROWS = 2048
STEP_X = 4

VMEM = pl.BlockSpec(memory_space=pltpu.VMEM)
SMEM = pl.BlockSpec(memory_space=pltpu.SMEM)
HBM = pl.BlockSpec(memory_space=pltpu.HBM)


def iota(shape, dim):
    return lax.broadcasted_iota(jnp.int32, shape, dim)


def shifted_lanes(v):
    lane = iota(v.shape, v.ndim - 1)
    before = jnp.where(lane == 0, 0.0, pltpu.roll(v, 1, v.ndim - 1))
    after = jnp.where(lane == CZ - 1, 0.0, pltpu.roll(v, CZ - 1, v.ndim - 1))
    return before + after


def pick(table, classes):
    low, mid, high = (classes & 1) == 1, (classes & 2) == 2, (classes & 4) == 4
    pairs = [jnp.where(low, table[2 * i + 1], table[2 * i]) for i in range(4)]
    return jnp.where(high, jnp.where(mid, pairs[3], pairs[2]), jnp.where(mid, pairs[1], pairs[0]))


def open_sides():
    sides = []
    for axis in ("span", "pitch", "chord"):
        position, size = lax.axis_index(axis), lax.axis_size(axis)
        sides.append(jnp.where(position > 0, 1.0, 0.0).astype(jnp.float32))
        sides.append(jnp.where(position < size - 1, 1.0, 0.0).astype(jnp.float32))
    return sides


def slots(shape):
    lane = iota(shape, len(shape) - 1)
    plane = (lane * 43) >> 8
    return plane, lane - 6 * plane


def column_kernel(
    table_in, start, source, classes, p0, cs, stiffness, z_low, z_high,
    table, y_in, s_in, c_in, beyond, sems, table_sem,
):
    table_copy = pltpu.make_async_copy(table_in, table, table_sem)
    table_copy.start()
    copies = []
    for g in range(CX // STEP_X):
        part = pl.ds(g * STEP_X, STEP_X)
        copies.append(
            [
                pltpu.make_async_copy(classes.at[part], c_in.at[part], sems.at[0, g]),
                pltpu.make_async_copy(start.at[:, part], y_in.at[:, part], sems.at[1, g]),
                pltpu.make_async_copy(source.at[:, part], s_in.at[:, part], sems.at[2, g]),
            ]
        )
        for copy in copies[-1]:
            copy.start()
    x_lo, x_hi, y_lo, y_hi, z_lo, z_hi = open_sides()

    lane = iota((CY, CZ), 1)
    edge = (lane < 3) | (lane >= CZ - 3)
    values = [jnp.zeros((CY, CZ), jnp.float32) for _ in range(3)]
    pushes = [jnp.zeros((CY, CZ), jnp.float32) for _ in range(3)]
    table_copy.wait()
    for x in range(CX):
        if x % STEP_X == 0:
            for copy in copies[x // STEP_X]:
                copy.wait()
        k = pick(table, c_in[x])
        stiffness[x] = k
        shift = (6 * (x + 2) + 3) % CZ
        for c in range(3):
            value = k * y_in[c, x]
            push = STEP * s_in[c, x]
            p0[c, x] = value
            cs[c, x] = push
            values[c] = values[c] + pltpu.roll(jnp.where(edge, value, 0.0), shift, 1)
            pushes[c] = pushes[c] + pltpu.roll(jnp.where(edge, push, 0.0), shift, 1)

    shape = (GY, CZ)
    plane, slot = slots(shape)
    row = iota(shape, 0)
    keep = jnp.where(row < 8, y_lo, jnp.where(row >= 8 + CY, y_hi, 1.0))
    side = jnp.where(plane < 2, x_lo, jnp.where(plane >= 2 + CX, x_hi, 1.0))
    side = jnp.where(plane < 20, side, 0.0) * keep
    at_high, at_low = slot == 2, slot == 3
    gate = jnp.where(at_high, z_hi, jnp.where(at_low, z_lo, 0.0))
    no_before, no_after = (slot == 0) | (slot == 3), (slot == 2) | (slot == 5)
    pad = jnp.zeros((8, CZ), jnp.float32)
    _, packed_slot = slots((HALF, CZ))

    for c in range(3):
        along = PULL[c][2]

        def flat(v):
            planes = pltpu.roll(v, 6, 1) + pltpu.roll(v, CZ - 6, 1)
            lines = pltpu.roll(v, 1, 0) + pltpu.roll(v, GY - 1, 0)
            return (OWN * v + PULL[c][0] * planes + PULL[c][1] * lines) * side

        def beside(v):
            before = jnp.where(no_before, 0.0, pltpu.roll(v, 1, 1))
            after = jnp.where(no_after, 0.0, pltpu.roll(v, CZ - 1, 1))
            return along * (before + after)

        v0 = jnp.concatenate([pad, values[c], pad], axis=0)
        push = jnp.concatenate([pad, pushes[c], pad], axis=0)
        t1 = flat(v0)
        v1 = t1 + beside(v0) + push
        t2 = flat(v1)
        v2 = t2 + beside(v1) + push + (along * along) * gate * v0
        out1 = along * gate * (flat(t1) + t2 + v2 + (along * along) * v0)
        out2 = (along * along) * gate * (2.0 * t1 + v1)
        out3 = (along * along * along) * gate * v0
        given = jnp.zeros(shape, jnp.float32)
        for far, out in ((1, out1), (2, out2), (3, out3)):
            given = given + pltpu.roll(jnp.where(at_low, out, 0.0), CZ - far, 1)
            given = given + pltpu.roll(jnp.where(at_high, out, 0.0), far, 1)
        beyond[c] = given
        top, rest = beyond[c, FIRST:MIDDLE, :], beyond[c, MIDDLE:LAST, :]
        rows = slice(HALF * c, HALF * (c + 1))
        z_low[rows, :] = jnp.where(packed_slot < 3, top, pltpu.roll(rest, 3, 1))
        z_high[rows, :] = jnp.where(packed_slot >= 3, rest, pltpu.roll(top, CZ - 3, 1))
    for out in (z_low, z_high):
        out[3 * HALF : 56, :] = jnp.zeros((56 - 3 * HALF, CZ), jnp.float32)


def sweep_kernel(p0_in, cs_in, inner, y_low, y_high, x_out, core, p0, p1, p2, q, cs):
    x_lo, x_hi, y_lo, y_hi, z_lo, z_hi = open_sides()
    shape = (GY, CZ)
    row, lane = iota(shape, 0), iota(shape, 1)
    keep = jnp.where(row < 8, y_lo, jnp.where(row >= 8 + CY, y_hi, 1.0))
    gate = jnp.where(lane == 0, z_lo, jnp.where(lane == CZ - 1, z_hi, 0.0))
    zeros = jnp.zeros(shape, jnp.float32)

    def clear(ref, planes):
        for c in range(3):
            for x in planes:
                ref[c, x] = zeros

    clear(p0, (2, 3, 20, 21))
    clear(p1, (1, 2, 21, 22))
    clear(p2, (0, 1, 22, 23))
    clear(q, (1, 2, 21, 22))
    clear(cs, (1, 2, 3, 20, 21, 22))
    pad = jnp.zeros((8, CZ), jnp.float32)
    for x in range(CX):
        for c in range(3):
            for ref, given in ((p0, p0_in), (cs, cs_in)):
                ref[c, x + 4, 0:8, :] = pad
                ref[c, x + 4, 8 : 8 + CY, :] = given[c, x]
                ref[c, x + 4, 8 + CY : GY, :] = pad

    def across(ref, c, x):
        here = ref[c, x]
        planes = ref[c, x - 1] + ref[c, x + 1]
        lines = pltpu.roll(here, 1, 0) + pltpu.roll(here, GY - 1, 0)
        side = jnp.where(x < 4, x_lo, jnp.where(x >= 4 + CX, x_hi, 1.0))
        return here, (OWN * here + PULL[c][0] * planes + PULL[c][1] * lines) * (keep * side)

    def first(x, carry):
        for c in range(3):
            here, flat = across(p0, c, x)
            new = flat + PULL[c][2] * shifted_lanes(here) + cs[c, x]
            p1[c, x] = new
            q[c, x] = flat + new
        return carry

    lax.fori_loop(3, 21, first, 0, unroll=True)

    def second(x, carry):
        for c in range(3):
            here, flat = across(p1, c, x)
            new = flat + PULL[c][2] * shifted_lanes(here) + cs[c, x]
            p2[c, x] = new + (PULL[c][2] * PULL[c][2] * gate) * p0[c, x]
        return carry

    lax.fori_loop(2, 22, second, 0, unroll=True)

    def third(x):
        values = []
        for c in range(3):
            here, flat = across(p2, c, x)
            new = flat + PULL[c][2] * shifted_lanes(here) + cs[c, x]
            new = new + (PULL[c][2] * PULL[c][2] * gate) * q[c, x]
            y_low[c, x] = new[0:8, :]
            y_high[c, x] = new[8 + CY : GY, :]
            values.append(new[8 : 8 + CY, :])
        return values

    for i, x in enumerate((1, 2, 3, 20, 21, 22)):
        for c, value in enumerate(third(x)):
            x_out[c, i] = value
            if i >= 3:
                core[c, i - 3] = value[8:24, :]

    def middle(x, carry):
        for c, value in enumerate(third(x)):
            inner[c, x - 4] = value
        return carry

    lax.fori_loop(4, 20, middle, 0, unroll=True)


def unpack(z_next, z_prev, columns):
    _, slot = slots((HALF, CZ))
    for c in range(3):
        rows = slice(HALF * c, HALF * (c + 1))
        above, below = z_next[rows, :], z_prev[rows, :]
        columns[c, 0:8, :] = jnp.zeros((8, CZ), jnp.float32)
        columns[c, GY - 8 : GY, :] = jnp.zeros((8, CZ), jnp.float32)
        columns[c, FIRST:MIDDLE, :] = jnp.where(slot < 3, above, pltpu.roll(below, 3, 1))
        columns[c, MIDDLE:LAST, :] = jnp.where(slot < 3, pltpu.roll(above, CZ - 3, 1), below)


def chord_part(columns, c, x, start, size):
    lane = iota((size, CZ), 1)
    placed = pltpu.roll(columns[c, start : start + size, :], (CZ - 3 - 6 * (x - 2)) % CZ, 1)
    return jnp.where((lane < 3) | (lane >= CZ - 3), placed, 0.0)


def pitch_kernel(y_low, y_high, z_next, z_prev, low, high, columns):
    unpack(z_next, z_prev, columns)
    for c in range(3):
        for x in range(1, 23):
            for tile, out, start, first in ((y_low, low, 0, 5), (y_high, high, 40, 0)):
                value = tile[c, x]
                if 2 <= x < 22:
                    value = value + chord_part(columns, c, x, start, 8)
                for j in range(3):
                    out[c, j, x : x + 1, :] = value[first + j : first + j + 1, :]


def pitch_rows(y_next, y_prev, c, x):
    row = iota((8, CZ), 0)
    bottom = jnp.zeros((8, CZ), jnp.float32)
    top = jnp.zeros((8, CZ), jnp.float32)
    for j in range(3):
        bottom = jnp.where(row == j, y_prev[c, j, x : x + 1, :], bottom)
        top = jnp.where(row == 5 + j, y_next[c, j, x : x + 1, :], top)
    return bottom, top


def span_kernel(x_out, z_next, z_prev, y_next, y_prev, low, high, columns):
    unpack(z_next, z_prev, columns)
    lane = iota((CY // 2, CZ), 1)
    packed = jnp.zeros((CY // 2, CZ), jnp.float32)
    for c in range(3):
        placed = pltpu.roll(columns[c, 16:32, :], 12 * c + CZ - 6 * 18, 1)
        packed = jnp.where((lane >= 12 * c) & (lane < 12 * (c + 1)), placed, packed)
    high[9] = packed
    for c in range(3):
        for i, x in enumerate((1, 2, 3, 20, 21, 22)):
            value = x_out[c, i]
            if 2 <= x < 22:
                value = value + chord_part(columns, c, x, 8, CY)
            bottom, top = pitch_rows(y_next, y_prev, c, x)
            if i < 3:
                low[c, i, 0:8, :] = value[0:8, :] + bottom
                low[c, i, 8:24, :] = value[8:24, :]
                low[c, i, 24:32, :] = value[24:32, :] + top
            else:
                high[3 * c + i - 3, 0:8, :] = value[0:8, :] + bottom
                high[3 * c + i - 3, 8:16, :] = value[24:32, :] + top


def finish_planes(planes, inner, z_next, z_prev, y_next, y_prev, stiffness, columns, values, part, field, span):
    unpack(z_next, z_prev, columns)
    zeros = jnp.zeros((8, CZ), jnp.float32)
    for i, x in enumerate(planes):
        ratio = 1.0 / stiffness[x]
        for c in range(3):
            value = inner[c, x] + chord_part(columns, c, x + 4, 8, CY)
            bottom, top = pitch_rows(y_next, y_prev, c, x + 4)
            value = value + jnp.concatenate([bottom, zeros, zeros, top], axis=0)
            value = span(value, c, x)
            values[c, i] = value * ratio
            part[c, CY * i : CY * (i + 1), :] = value
    for c in range(3):
        for g in range(CY * len(planes) // 128):
            block = part[c, 128 * g : 128 * (g + 1), :].T
            first = block.astype(jnp.bfloat16)
            second = (block - first.astype(jnp.float32)).astype(jnp.bfloat16)
            field[256 * c : 256 * c + 128, 128 * g : 128 * (g + 1)] = first
            field[256 * c + 128 : 256 * c + 256, 128 * g : 128 * (g + 1)] = second


def marks(length, place):
    return (iota((length, place.shape[1]), 0) == place).astype(jnp.bfloat16)


def mark_kernel(wall_cell, patch_owner, after, planes, patches):
    for step in range(WALL // 512):
        here = slice(step * 512, (step + 1) * 512)
        plane = wall_cell[:, here] >> 7
        place = jnp.where(plane < 128, plane, jnp.where(plane >= 384, plane - 256, -1))
        planes[:, here] = marks(256, place)
        patches[here, :] = marks(PATCH_DEV, patch_owner[:, here] & 127).T


def normal_share(field, planes, cell, normals):
    count = cell.shape[1]
    picked = jnp.dot(field[...], planes, preferred_element_type=jnp.float32)
    value = jnp.zeros((CZ, count), jnp.float32)
    for c in range(3):
        part = picked[256 * c : 256 * c + 128] + picked[256 * c + 128 : 256 * c + 256]
        value = value + normals[c : c + 1] * part
    value = jnp.where(iota((CZ, count), 0) == (cell & 127), value, 0.0)
    return jnp.sum(value, axis=0, keepdims=True)


def middle_kernel(
    inner, stiffness, z_next, z_prev, y_next, y_prev, wall_cell, wall_normal,
    adjoint, share, columns, values, part, field, sem,
):
    def as_is(value, c, x):
        return value

    finish_planes(
        range(4, 12), inner, z_next, z_prev, y_next, y_prev,
        stiffness, columns, values, part, field, as_is,
    )
    copy = pltpu.make_async_copy(values, adjoint.at[:, 4:12], sem)
    copy.start()
    for step in range(WALL // ROWS):
        here = slice(step * ROWS, (step + 1) * ROWS)
        cell = wall_cell[:, here]
        share[:, here] = normal_share(
            field, marks(256, (cell >> 7) - 128), cell, wall_normal[:, here]
        )
    copy.wait()


def wall_kernel(
    given, inner, stiffness, z_next, z_prev, y_next, y_prev, x_next, x_prev, x_core, share,
    wall_cell, patch_owner, wall_normal, mode_shape, planes, patches,
    adjoint, sums, columns, values, part, field, sems,
):
    def span(value, c, x):
        if x < 3:
            rows = x_core[c, x]
            if x < 2:
                lane = iota(rows.shape, 1)
                placed = pltpu.roll(x_prev[9], CZ - 3 - 12 * c - 6 * x, 1)
                rows = rows + jnp.where((lane < 3) | (lane >= CZ - 3), placed, 0.0)
            parts = [x_prev[3 * c + x, 0:8, :], rows, x_prev[3 * c + x, 8:16, :]]
            return value + jnp.concatenate(parts, axis=0)
        if x >= CX - 3:
            return value + x_next[c, x - (CX - 3)]
        return value

    finish_planes(
        (0, 1, 2, 3, 12, 13, 14, 15), inner, z_next, z_prev, y_next, y_prev,
        stiffness, columns, values, part, field, span,
    )
    copies = [
        pltpu.make_async_copy(values.at[:, 0:4], adjoint.at[:, 0:4], sems.at[0]),
        pltpu.make_async_copy(values.at[:, 4:8], adjoint.at[:, 12:16], sems.at[1]),
    ]
    for copy in copies:
        copy.start()
    total = jnp.zeros((2 * CHORD * MODES, PATCH_DEV), jnp.float32)
    for step in range(WALL // ROWS):
        here = slice(step * ROWS, (step + 1) * ROWS)
        cell, owner = wall_cell[:, here], patch_owner[:, here]
        normal = share[:, here] + normal_share(field, planes[:, here], cell, wall_normal[:, here])
        parts = mode_shape[:, here] * normal
        high = parts.astype(jnp.bfloat16).astype(jnp.float32)
        pieces = jnp.concatenate([high, parts - high], axis=0).astype(jnp.bfloat16)
        device = jnp.broadcast_to((owner >> 7).astype(jnp.float32), pieces.shape).astype(jnp.bfloat16)
        both = jnp.concatenate(
            [jnp.where(device == o, pieces, jnp.bfloat16(0)) for o in range(CHORD)], axis=0
        )
        total = total + jnp.dot(both, patches[here, :], preferred_element_type=jnp.float32)
    for o in range(CHORD):
        first, second = 2 * MODES * o, MODES * (2 * o + 1)
        sums[MODES * o : MODES * (o + 1), :] = total[first : first + MODES] + total[second : second + MODES]
    for copy in copies:
        copy.wait()


def call(
    kernel, outs, operands, spaces, scratch=(), out_spaces=None, aliases=None, flops=0, kind=jnp.float32
):
    spec = {"h": HBM, "s": SMEM, "v": VMEM}
    shapes = tuple(jax.ShapeDtypeStruct(shape, kind) for shape in outs)
    moved = sum(4 * o.size for o in operands) + sum(4 * s.size for s in shapes)
    operands = [
        pltpu.with_memory_space_constraint(o, pltpu.HBM) if space == "h" else o
        for o, space in zip(operands, spaces)
    ]
    return pl.pallas_call(
        kernel,
        out_shape=shapes,
        in_specs=[spec[space] for space in spaces],
        out_specs=tuple(spec[space] for space in out_spaces or "v" * len(outs)),
        scratch_shapes=list(scratch),
        input_output_aliases=aliases or {},
        cost_estimate=pl.CostEstimate(flops=flops, bytes_accessed=moved, transcendentals=0),
        compiler_params=pltpu.CompilerParams(vmem_limit_bytes=40 << 20),
    )(*operands)


def pairs(axis):
    return [(i, i + 1) for i in range(lax.axis_size(axis) - 1)]


def from_next(low, axis):
    return lax.ppermute(low, axis, [(j, i) for i, j in pairs(axis)])


def from_previous(high, axis):
    return lax.ppermute(high, axis, pairs(axis))


def body(
    adjoint_start,
    sensitivity_source,
    stiffness_class,
    stiffness_table,
    wall_cell,
    patch_owner,
    wall_normal,
    mode_shape,
):
    block, columns = (3, CX, CY, CZ), pltpu.VMEM((3, GY, CZ), jnp.float32)
    grown = pltpu.VMEM((3, GX, GY, CZ), jnp.float32)
    p0, cs, stiffness, z_low, z_high = call(
        column_kernel,
        (block, block, (CX, CY, CZ), (56, CZ), (56, CZ)),
        (stiffness_table, adjoint_start, sensitivity_source, stiffness_class),
        "hhhh",
        scratch=(
            pltpu.SMEM((8,), jnp.float32),
            pltpu.VMEM(block, jnp.float32),
            pltpu.VMEM(block, jnp.float32),
            pltpu.VMEM((CX, CY, CZ), jnp.int32),
            columns,
            pltpu.SemaphoreType.DMA((3, CX // STEP_X)),
            pltpu.SemaphoreType.DMA,
        ),
    )
    z_prev, z_next = from_previous(z_high, "chord"), from_next(z_low, "chord")
    inner, y_low, y_high, x_out, core = call(
        sweep_kernel,
        (block, (3, GX, 8, CZ), (3, GX, 8, CZ), (3, 6, CY, CZ), (3, 3, CY // 2, CZ)),
        (p0, cs),
        "vv",
        scratch=(grown,) * 5,
        flops=1 << 25,
    )
    cells, owners = wall_cell.reshape(1, WALL), patch_owner.reshape(1, WALL)
    planes, patches = call(
        mark_kernel,
        ((256, WALL), (WALL, PATCH_DEV)),
        (cells, owners, y_low),
        "vvv",
        flops=1 << 25,
        kind=jnp.bfloat16,
    )
    y_low, planes, patches = lax.optimization_barrier((y_low, planes, patches))
    slab = (3, 3, GX, CZ)
    low, high = call(
        pitch_kernel, (slab, slab), (y_low, y_high, z_next, z_prev), "vvvv", scratch=(columns,)
    )
    x_core = from_previous(core, "span")
    y_next, y_prev = from_next(low, "pitch"), from_previous(high, "pitch")
    y_next, y_prev, x_core = lax.optimization_barrier((y_next, y_prev, x_core))
    low, high = call(
        span_kernel,
        ((3, 3, CY, CZ), (10, CY // 2, CZ)),
        (x_out, z_next, z_prev, y_next, y_prev),
        "vvvvv",
        scratch=(columns,),
    )
    x_next, x_prev = from_next(low, "span"), from_previous(high, "span")
    given = (z_next, z_prev, y_next, y_prev)
    work = (
        columns,
        pltpu.VMEM((3, CX // 2, CY, CZ), jnp.float32),
        pltpu.VMEM((3, CX // 2 * CY, CZ), jnp.float32),
        pltpu.VMEM((6 * CZ, CX // 2 * CY), jnp.bfloat16),
    )
    adjoint, share = call(
        middle_kernel,
        (block, (1, WALL)),
        (inner, stiffness, *given, cells, wall_normal),
        "vvvvvvvv",
        scratch=(*work, pltpu.SemaphoreType.DMA),
        out_spaces="hv",
        flops=1 << 30,
    )
    adjoint, sums = call(
        wall_kernel,
        (block, (CHORD * MODES, PATCH_DEV)),
        (
            adjoint, inner, stiffness, *given, x_next, x_prev, x_core, share,
            cells, owners, wall_normal, mode_shape, planes, patches,
        ),
        "hvvvvvvvvvvvvvvvv",
        scratch=(*work, pltpu.SemaphoreType.DMA((2,))),
        out_spaces="hv",
        aliases={0: 0},
        flops=1 << 30,
    )
    sums = sums.reshape(CHORD, MODES, PATCH_DEV)
    arrived = lax.all_to_all(sums, "chord", split_axis=0, concat_axis=0, tiled=True)
    return adjoint, arrived.sum(axis=0)


def solution(mesh):
    in_specs = (
        P(None, "span", "pitch", "chord"),
        P(None, "span", "pitch", "chord"),
        P("span", "pitch", "chord"),
        P(),
        P(("span", "pitch", "chord")),
        P(("span", "pitch", "chord"), None),
        P(None, ("span", "pitch", "chord")),
        P(None, ("span", "pitch", "chord")),
    )
    out_specs = (P(None, "span", "pitch", "chord"), P(None, ("span", "pitch", "chord")))
    return jax.shard_map(body, mesh=mesh, in_specs=in_specs, out_specs=out_specs, check_vma=False)
```

```python
import functools

import jax
import jax.numpy as jnp
from jax import lax
from jax.experimental import pallas as pl
from jax.experimental.pallas import tpu as pltpu
from jax.sharding import PartitionSpec as P

CX, CY, CZ = 16, 32, 128
PATCH_DEV = 128
MODES = 8
CHORD = 16
WALL = 4096

MASS_SHIFT = 0.5
RELAXATION = 0.8
DIAGONAL_SUM = 10.5
LAME_WEIGHTS = ((3.0, 1.0, 1.0), (1.0, 3.0, 1.0), (1.0, 1.0, 3.0))

STEP = RELAXATION / DIAGONAL_SUM
OWN = 1.0 - STEP * (MASS_SHIFT + 2.0 * sum(LAME_WEIGHTS[0]))
PULL = tuple(tuple(STEP * weight for weight in row) for row in LAME_WEIGHTS)

GX, GY = 24, 48
FIRST, MIDDLE, LAST = 6, 24, 42
HALF = MIDDLE - FIRST
SLAB = 168
ROWS = 2048
STEP_X = 8

VMEM = pl.BlockSpec(memory_space=pltpu.VMEM)
SMEM = pl.BlockSpec(memory_space=pltpu.SMEM)
HBM = pl.BlockSpec(memory_space=pltpu.HBM)


def iota(shape, dim):
    return lax.broadcasted_iota(jnp.int32, shape, dim)


def shifted_lanes(v):
    lane = iota(v.shape, v.ndim - 1)
    before = jnp.where(lane == 0, 0.0, pltpu.roll(v, 1, v.ndim - 1))
    after = jnp.where(lane == CZ - 1, 0.0, pltpu.roll(v, CZ - 1, v.ndim - 1))
    return before + after


def pick(table, classes):
    low, mid, high = (classes & 1) == 1, (classes & 2) == 2, (classes & 4) == 4
    pairs = [jnp.where(low, table[2 * i + 1], table[2 * i]) for i in range(4)]
    return jnp.where(high, jnp.where(mid, pairs[3], pairs[2]), jnp.where(mid, pairs[1], pairs[0]))


def open_sides():
    sides = []
    for axis in ("span", "pitch", "chord"):
        position, size = lax.axis_index(axis), lax.axis_size(axis)
        sides.append(jnp.where(position > 0, 1.0, 0.0).astype(jnp.float32))
        sides.append(jnp.where(position < size - 1, 1.0, 0.0).astype(jnp.float32))
    return sides


def slots(shape):
    lane = iota(shape, len(shape) - 1)
    plane = (lane * 43) >> 8
    return plane, lane - 6 * plane


def column_kernel(
    table_in, start, source, classes, p0, cs, stiffness, z_low, z_high,
    table, y_in, s_in, c_in, beyond, sems, table_sem,
):
    table_copy = pltpu.make_async_copy(table_in, table, table_sem)
    table_copy.start()
    early, late = [], []
    for g in range(CX // STEP_X):
        part = pl.ds(g * STEP_X, STEP_X)
        early.append(
            [
                pltpu.make_async_copy(classes.at[part], c_in.at[part], sems.at[0, g]),
                pltpu.make_async_copy(start.at[:, part], y_in.at[:, part], sems.at[1, g]),
            ]
        )
        late.append(pltpu.make_async_copy(source.at[:, part], s_in.at[:, part], sems.at[2, g]))
    for copy in [copy for group in early for copy in group] + late:
        copy.start()
    x_lo, x_hi, y_lo, y_hi, z_lo, z_hi = open_sides()

    lane = iota((CY, CZ), 1)
    edge = (lane < 3) | (lane >= CZ - 3)
    values = [jnp.zeros((CY, CZ), jnp.float32) for _ in range(3)]
    pushes = [jnp.zeros((CY, CZ), jnp.float32) for _ in range(3)]
    table_copy.wait()
    for x in range(CX):
        if x % STEP_X == 0:
            for copy in early[x // STEP_X]:
                copy.wait()
        k = pick(table, c_in[x])
        stiffness[x] = k
        for c in range(3):
            value = k * y_in[c, x]
            p0[c, x] = value
            values[c] = values[c] + pltpu.roll(jnp.where(edge, value, 0.0), (6 * (x + 2) + 3) % CZ, 1)

    shape = (GY, CZ)
    plane, slot = slots(shape)
    row = iota(shape, 0)
    keep = jnp.where(row < 8, y_lo, jnp.where(row >= 8 + CY, y_hi, 1.0))
    side = jnp.where(plane < 2, x_lo, jnp.where(plane >= 2 + CX, x_hi, 1.0))
    side = jnp.where(plane < 20, side, 0.0) * keep
    at_high, at_low = slot == 2, slot == 3
    gate = jnp.where(at_high, z_hi, jnp.where(at_low, z_lo, 0.0))
    no_before, no_after = (slot == 0) | (slot == 3), (slot == 2) | (slot == 5)
    pad = jnp.zeros((8, CZ), jnp.float32)
    _, packed_slot = slots((HALF, CZ))

    def flat(v, c):
        planes = pltpu.roll(v, 6, 1) + pltpu.roll(v, CZ - 6, 1)
        lines = pltpu.roll(v, 1, 0) + pltpu.roll(v, GY - 1, 0)
        return (OWN * v + PULL[c][0] * planes + PULL[c][1] * lines) * side

    def beside(v, c):
        before = jnp.where(no_before, 0.0, pltpu.roll(v, 1, 1))
        after = jnp.where(no_after, 0.0, pltpu.roll(v, CZ - 1, 1))
        return PULL[c][2] * (before + after)

    v0s = [jnp.concatenate([pad, values[c], pad], axis=0) for c in range(3)]
    t1s = [flat(v0s[c], c) for c in range(3)]
    unpushed = [t1s[c] + beside(v0s[c], c) for c in range(3)]
    twice = [flat(t1s[c], c) for c in range(3)]

    for x in range(CX):
        if x % STEP_X == 0:
            late[x // STEP_X].wait()
        for c in range(3):
            push = STEP * s_in[c, x]
            cs[c, x] = push
            pushes[c] = pushes[c] + pltpu.roll(jnp.where(edge, push, 0.0), (6 * (x + 2) + 3) % CZ, 1)

    for c in range(3):
        along = PULL[c][2]
        v0, t1 = v0s[c], t1s[c]
        push = jnp.concatenate([pad, pushes[c], pad], axis=0)
        v1 = unpushed[c] + push
        t2 = flat(v1, c)
        v2 = t2 + beside(v1, c) + push + (along * along) * gate * v0
        out1 = along * gate * (twice[c] + t2 + v2 + (along * along) * v0)
        out2 = (along * along) * gate * (2.0 * t1 + v1)
        out3 = (along * along * along) * gate * v0
        given = jnp.zeros(shape, jnp.float32)
        for far, out in ((1, out1), (2, out2), (3, out3)):
            given = given + pltpu.roll(jnp.where(at_low, out, 0.0), CZ - far, 1)
            given = given + pltpu.roll(jnp.where(at_high, out, 0.0), far, 1)
        beyond[c] = given
        top, rest = beyond[c, FIRST:MIDDLE, :], beyond[c, MIDDLE:LAST, :]
        rows = slice(HALF * c, HALF * (c + 1))
        z_low[rows, :] = jnp.where(packed_slot < 3, top, pltpu.roll(rest, 3, 1))
        z_high[rows, :] = jnp.where(packed_slot >= 3, rest, pltpu.roll(top, CZ - 3, 1))
    for out in (z_low, z_high):
        out[3 * HALF : 56, :] = jnp.zeros((56 - 3 * HALF, CZ), jnp.float32)


def sweep_kernel(p0_in, cs_in, inner, y_low, y_high, x_out, p0, p1, p2, q, cs):
    x_lo, x_hi, y_lo, y_hi, z_lo, z_hi = open_sides()
    shape = (GY, CZ)
    row, lane = iota(shape, 0), iota(shape, 1)
    keep = jnp.where(row < 8, y_lo, jnp.where(row >= 8 + CY, y_hi, 1.0))
    gate = jnp.where(lane == 0, z_lo, jnp.where(lane == CZ - 1, z_hi, 0.0))
    zeros = jnp.zeros(shape, jnp.float32)

    def clear(ref, planes):
        for c in range(3):
            for x in planes:
                ref[c, x] = zeros

    clear(p0, (2, 3, 20, 21))
    clear(p1, (1, 2, 21, 22))
    clear(p2, (0, 1, 22, 23))
    clear(q, (1, 2, 21, 22))
    clear(cs, (1, 2, 3, 20, 21, 22))
    pad = jnp.zeros((8, CZ), jnp.float32)
    for x in range(CX):
        for c in range(3):
            for ref, given in ((p0, p0_in), (cs, cs_in)):
                ref[c, x + 4, 0:8, :] = pad
                ref[c, x + 4, 8 : 8 + CY, :] = given[c, x]
                ref[c, x + 4, 8 + CY : GY, :] = pad

    def across(ref, c, x):
        here = ref[c, x]
        planes = ref[c, x - 1] + ref[c, x + 1]
        lines = pltpu.roll(here, 1, 0) + pltpu.roll(here, GY - 1, 0)
        side = jnp.where(x < 4, x_lo, jnp.where(x >= 4 + CX, x_hi, 1.0))
        return here, (OWN * here + PULL[c][0] * planes + PULL[c][1] * lines) * (keep * side)

    def first(x, carry):
        for c in range(3):
            here, flat = across(p0, c, x)
            new = flat + PULL[c][2] * shifted_lanes(here) + cs[c, x]
            p1[c, x] = new
            q[c, x] = flat + new
        return carry

    lax.fori_loop(3, 21, first, 0, unroll=True)

    def second(x, carry):
        for c in range(3):
            here, flat = across(p1, c, x)
            new = flat + PULL[c][2] * shifted_lanes(here) + cs[c, x]
            p2[c, x] = new + (PULL[c][2] * PULL[c][2] * gate) * p0[c, x]
        return carry

    lax.fori_loop(2, 22, second, 0, unroll=True)

    def third(x):
        values = []
        for c in range(3):
            here, flat = across(p2, c, x)
            new = flat + PULL[c][2] * shifted_lanes(here) + cs[c, x]
            new = new + (PULL[c][2] * PULL[c][2] * gate) * q[c, x]
            y_low[c, x] = new[0:8, :]
            y_high[c, x] = new[8 + CY : GY, :]
            values.append(new[8 : 8 + CY, :])
        return values

    for i, x in enumerate((1, 2, 3, 20, 21, 22)):
        for c, value in enumerate(third(x)):
            x_out[c, i] = value

    def middle(x, carry):
        for c, value in enumerate(third(x)):
            inner[c, x - 4] = value
        return carry

    lax.fori_loop(4, 20, middle, 0, unroll=True)


def unpack(z_next, z_prev, columns):
    _, slot = slots((HALF, CZ))
    for c in range(3):
        rows = slice(HALF * c, HALF * (c + 1))
        above, below = z_next[rows, :], z_prev[rows, :]
        columns[c, 0:8, :] = jnp.zeros((8, CZ), jnp.float32)
        columns[c, GY - 8 : GY, :] = jnp.zeros((8, CZ), jnp.float32)
        columns[c, FIRST:MIDDLE, :] = jnp.where(slot < 3, above, pltpu.roll(below, 3, 1))
        columns[c, MIDDLE:LAST, :] = jnp.where(slot < 3, pltpu.roll(above, CZ - 3, 1), below)


def chord_part(columns, c, x, start, size):
    lane = iota((size, CZ), 1)
    placed = pltpu.roll(columns[c, start : start + size, :], (CZ - 3 - 6 * (x - 2)) % CZ, 1)
    return jnp.where((lane < 3) | (lane >= CZ - 3), placed, 0.0)


def slab_row(c, far, x):
    place = x - (1 + far)
    count = 22 - 2 * far
    return 54 * c + (0, 20, 38)[far - 1] + place if 0 <= place < count else None


def pitch_kernel(y_low, y_high, z_next, z_prev, low, high, columns):
    unpack(z_next, z_prev, columns)
    for c in range(3):
        for x in range(1, 23):
            for tile, out, start, first in ((y_low, low, 0, 5), (y_high, high, 40, 0)):
                value = tile[c, x]
                if 2 <= x < 22:
                    value = value + chord_part(columns, c, x, start, 8)
                for j in range(3):
                    far = 3 - j if first else j + 1
                    place = slab_row(c, far, x)
                    if place is not None:
                        out[place : place + 1, :] = value[first + j : first + j + 1, :]
    for out in (low, high):
        out[SLAB - 6 : SLAB, :] = jnp.zeros((6, CZ), jnp.float32)


def pitch_rows(y_next, y_prev, c, x):
    row = iota((8, CZ), 0)
    bottom = jnp.zeros((8, CZ), jnp.float32)
    top = jnp.zeros((8, CZ), jnp.float32)
    for j in range(3):
        low, high = slab_row(c, j + 1, x), slab_row(c, 3 - j, x)
        if low is not None:
            bottom = jnp.where(row == j, y_prev[low : low + 1, :], bottom)
        if high is not None:
            top = jnp.where(row == 5 + j, y_next[high : high + 1, :], top)
    return bottom, top


def span_kernel(x_out, z_next, z_prev, y_next, y_prev, low, high, columns):
    unpack(z_next, z_prev, columns)
    for c in range(3):
        for i, x in enumerate((1, 2, 3, 20, 21, 22)):
            out, j = (low, i) if i < 3 else (high, i - 3)
            value = x_out[c, i]
            if 2 <= x < 22:
                value = value + chord_part(columns, c, x, 8, CY)
            out[c, j] = value
            bottom, top = pitch_rows(y_next, y_prev, c, x)
            out[c, j, 0:8, :] += bottom
            out[c, j, 24:32, :] += top


def finish_planes(planes, inner, z_next, z_prev, y_next, y_prev, stiffness, columns, values, part, field, span):
    unpack(z_next, z_prev, columns)
    zeros = jnp.zeros((8, CZ), jnp.float32)
    for i, x in enumerate(planes):
        ratio = 1.0 / stiffness[x]
        for c in range(3):
            value = inner[c, x] + chord_part(columns, c, x + 4, 8, CY)
            bottom, top = pitch_rows(y_next, y_prev, c, x + 4)
            value = value + jnp.concatenate([bottom, zeros, zeros, top], axis=0)
            value = span(value, c, x)
            values[c, i] = value * ratio
            part[c, CY * i : CY * (i + 1), :] = value
    for c in range(3):
        for g in range(CY * len(planes) // 128):
            block = part[c, 128 * g : 128 * (g + 1), :].T
            first = block.astype(jnp.bfloat16)
            second = (block - first.astype(jnp.float32)).astype(jnp.bfloat16)
            field[256 * c : 256 * c + 128, 128 * g : 128 * (g + 1)] = first
            field[256 * c + 128 : 256 * c + 256, 128 * g : 128 * (g + 1)] = second


def marks(length, place):
    return (iota((length, place.shape[1]), 0) == place).astype(jnp.bfloat16)


def mark_kernel(wall_cell, patch_owner, after, planes, patches):
    for step in range(WALL // 512):
        here = slice(step * 512, (step + 1) * 512)
        plane = wall_cell[:, here] >> 7
        place = jnp.where(plane < 128, plane, jnp.where(plane >= 384, plane - 256, -1))
        planes[:, here] = marks(256, place)
        patches[here, :] = marks(PATCH_DEV, patch_owner[:, here] & 127).T


def normal_share(field, planes, cell, normals):
    count = cell.shape[1]
    picked = jnp.dot(field[...], planes, preferred_element_type=jnp.float32)
    value = jnp.zeros((CZ, count), jnp.float32)
    for c in range(3):
        part = picked[256 * c : 256 * c + 128] + picked[256 * c + 128 : 256 * c + 256]
        value = value + normals[c : c + 1] * part
    value = jnp.where(iota((CZ, count), 0) == (cell & 127), value, 0.0)
    return jnp.sum(value, axis=0, keepdims=True)


def middle_kernel(
    inner, stiffness, z_next, z_prev, y_next, y_prev, wall_cell, wall_normal,
    adjoint, share, columns, values, part, field, sem,
):
    def as_is(value, c, x):
        return value

    finish_planes(
        range(4, 12), inner, z_next, z_prev, y_next, y_prev,
        stiffness, columns, values, part, field, as_is,
    )
    copy = pltpu.make_async_copy(values, adjoint.at[:, 4:12], sem)
    copy.start()
    for step in range(WALL // ROWS):
        here = slice(step * ROWS, (step + 1) * ROWS)
        cell = wall_cell[:, here]
        share[:, here] = normal_share(
            field, marks(256, (cell >> 7) - 128), cell, wall_normal[:, here]
        )
    copy.wait()


def wall_kernel(
    given, inner, stiffness, z_next, z_prev, y_next, y_prev, x_next, x_prev, share,
    wall_cell, patch_owner, wall_normal, mode_shape, planes, patches,
    adjoint, sums, columns, values, part, field, sems,
):
    def span(value, c, x):
        if x < 3:
            return value + x_prev[c, x]
        if x >= CX - 3:
            return value + x_next[c, x - (CX - 3)]
        return value

    finish_planes(
        (0, 1, 2, 3, 12, 13, 14, 15), inner, z_next, z_prev, y_next, y_prev,
        stiffness, columns, values, part, field, span,
    )
    copies = [
        pltpu.make_async_copy(values.at[:, 0:4], adjoint.at[:, 0:4], sems.at[0]),
        pltpu.make_async_copy(values.at[:, 4:8], adjoint.at[:, 12:16], sems.at[1]),
    ]
    for copy in copies:
        copy.start()
    total = jnp.zeros((2 * CHORD * MODES, PATCH_DEV), jnp.float32)
    for step in range(WALL // ROWS):
        here = slice(step * ROWS, (step + 1) * ROWS)
        cell, owner = wall_cell[:, here], patch_owner[:, here]
        normal = share[:, here] + normal_share(field, planes[:, here], cell, wall_normal[:, here])
        parts = mode_shape[:, here] * normal
        high = parts.astype(jnp.bfloat16).astype(jnp.float32)
        pieces = jnp.concatenate([high, parts - high], axis=0).astype(jnp.bfloat16)
        device = jnp.broadcast_to((owner >> 7).astype(jnp.float32), pieces.shape).astype(jnp.bfloat16)
        both = jnp.concatenate(
            [jnp.where(device == o, pieces, jnp.bfloat16(0)) for o in range(CHORD)], axis=0
        )
        total = total + jnp.dot(both, patches[here, :], preferred_element_type=jnp.float32)
    for o in range(CHORD):
        first, second = 2 * MODES * o, MODES * (2 * o + 1)
        sums[MODES * o : MODES * (o + 1), :] = total[first : first + MODES] + total[second : second + MODES]
    for copy in copies:
        copy.wait()


def call(
    kernel, outs, operands, spaces, scratch=(), out_spaces=None, aliases=None, flops=0, kind=jnp.float32
):
    spec = {"h": HBM, "s": SMEM, "v": VMEM}
    shapes = tuple(jax.ShapeDtypeStruct(shape, kind) for shape in outs)
    moved = sum(4 * o.size for o in operands) + sum(4 * s.size for s in shapes)
    operands = [
        pltpu.with_memory_space_constraint(o, pltpu.HBM) if space == "h" else o
        for o, space in zip(operands, spaces)
    ]
    return pl.pallas_call(
        kernel,
        out_shape=shapes,
        in_specs=[spec[space] for space in spaces],
        out_specs=tuple(spec[space] for space in out_spaces or "v" * len(outs)),
        scratch_shapes=list(scratch),
        input_output_aliases=aliases or {},
        cost_estimate=pl.CostEstimate(flops=flops, bytes_accessed=moved, transcendentals=0),
        compiler_params=pltpu.CompilerParams(vmem_limit_bytes=40 << 20),
    )(*operands)


def pairs(axis):
    return [(i, i + 1) for i in range(lax.axis_size(axis) - 1)]


def from_next(low, axis):
    return lax.ppermute(low, axis, [(j, i) for i, j in pairs(axis)])


def from_previous(high, axis):
    return lax.ppermute(high, axis, pairs(axis))


def body(
    adjoint_start,
    sensitivity_source,
    stiffness_class,
    stiffness_table,
    wall_cell,
    patch_owner,
    wall_normal,
    mode_shape,
):
    block, columns = (3, CX, CY, CZ), pltpu.VMEM((3, GY, CZ), jnp.float32)
    grown = pltpu.VMEM((3, GX, GY, CZ), jnp.float32)
    p0, cs, stiffness, z_low, z_high = call(
        column_kernel,
        (block, block, (CX, CY, CZ), (56, CZ), (56, CZ)),
        (stiffness_table, adjoint_start, sensitivity_source, stiffness_class),
        "hhhh",
        scratch=(
            pltpu.SMEM((8,), jnp.float32),
            pltpu.VMEM(block, jnp.float32),
            pltpu.VMEM(block, jnp.float32),
            pltpu.VMEM((CX, CY, CZ), jnp.int32),
            columns,
            pltpu.SemaphoreType.DMA((3, CX // STEP_X)),
            pltpu.SemaphoreType.DMA,
        ),
    )
    z_prev, z_next = from_previous(z_high, "chord"), from_next(z_low, "chord")
    inner, y_low, y_high, x_out = call(
        sweep_kernel,
        (block, (3, GX, 8, CZ), (3, GX, 8, CZ), (3, 6, CY, CZ)),
        (p0, cs),
        "vv",
        scratch=(grown,) * 5,
        flops=1 << 25,
    )
    cells, owners = wall_cell.reshape(1, WALL), patch_owner.reshape(1, WALL)
    planes, patches = call(
        mark_kernel,
        ((256, WALL), (WALL, PATCH_DEV)),
        (cells, owners, y_low),
        "vvv",
        flops=1 << 25,
        kind=jnp.bfloat16,
    )
    y_low, planes, patches = lax.optimization_barrier((y_low, planes, patches))
    slab = (SLAB, CZ)
    low, high = call(
        pitch_kernel, (slab, slab), (y_low, y_high, z_next, z_prev), "vvvv", scratch=(columns,)
    )
    y_next, y_prev = from_next(low, "pitch"), from_previous(high, "pitch")
    slab = (3, 3, CY, CZ)
    low, high = call(
        span_kernel, (slab, slab), (x_out, z_next, z_prev, y_next, y_prev), "vvvvv", scratch=(columns,)
    )
    x_next, x_prev = from_next(low, "span"), from_previous(high, "span")
    given = (z_next, z_prev, y_next, y_prev)
    work = (
        columns,
        pltpu.VMEM((3, CX // 2, CY, CZ), jnp.float32),
        pltpu.VMEM((3, CX // 2 * CY, CZ), jnp.float32),
        pltpu.VMEM((6 * CZ, CX // 2 * CY), jnp.bfloat16),
    )
    adjoint, share = call(
        middle_kernel,
        (block, (1, WALL)),
        (inner, stiffness, *given, cells, wall_normal),
        "vvvvvvvv",
        scratch=(*work, pltpu.SemaphoreType.DMA),
        out_spaces="hv",
        flops=1 << 30,
    )
    adjoint, sums = call(
        wall_kernel,
        (block, (CHORD * MODES, PATCH_DEV)),
        (
            adjoint, inner, stiffness, *given, x_next, x_prev, share,
            cells, owners, wall_normal, mode_shape, planes, patches,
        ),
        "hvvvvvvvvvvvvvvv",
        scratch=(*work, pltpu.SemaphoreType.DMA((2,))),
        out_spaces="hv",
        aliases={0: 0},
        flops=1 << 30,
    )
    sums = sums.reshape(CHORD, MODES, PATCH_DEV)
    arrived = lax.all_to_all(sums, "chord", split_axis=0, concat_axis=0, tiled=True)
    return adjoint, arrived.sum(axis=0)


def solution(mesh):
    in_specs = (
        P(None, "span", "pitch", "chord"),
        P(None, "span", "pitch", "chord"),
        P("span", "pitch", "chord"),
        P(),
        P(("span", "pitch", "chord")),
        P(("span", "pitch", "chord"), None),
        P(None, ("span", "pitch", "chord")),
        P(None, ("span", "pitch", "chord")),
    )
    out_specs = (P(None, "span", "pitch", "chord"), P(None, ("span", "pitch", "chord")))
    return jax.shard_map(body, mesh=mesh, in_specs=in_specs, out_specs=out_specs, check_vma=False)
```

```python
import functools

import jax
import jax.numpy as jnp
from jax import lax
from jax.experimental import pallas as pl
from jax.experimental.pallas import tpu as pltpu
from jax.sharding import PartitionSpec as P

CX, CY, CZ = 16, 32, 128
PATCH_DEV = 128
MODES = 8
CHORD = 16
WALL = 4096

MASS_SHIFT = 0.5
RELAXATION = 0.8
DIAGONAL_SUM = 10.5
LAME_WEIGHTS = ((3.0, 1.0, 1.0), (1.0, 3.0, 1.0), (1.0, 1.0, 3.0))

STEP = RELAXATION / DIAGONAL_SUM
OWN = 1.0 - STEP * (MASS_SHIFT + 2.0 * sum(LAME_WEIGHTS[0]))
PULL = tuple(tuple(STEP * weight for weight in row) for row in LAME_WEIGHTS)

GX, GY = 24, 48
FIRST, MIDDLE, LAST = 6, 24, 42
HALF = MIDDLE - FIRST
ROWS = 2048
STEP_X = 4

VMEM = pl.BlockSpec(memory_space=pltpu.VMEM)
SMEM = pl.BlockSpec(memory_space=pltpu.SMEM)
HBM = pl.BlockSpec(memory_space=pltpu.HBM)


def iota(shape, dim):
    return lax.broadcasted_iota(jnp.int32, shape, dim)


def shifted_lanes(v):
    lane = iota(v.shape, v.ndim - 1)
    before = jnp.where(lane == 0, 0.0, pltpu.roll(v, 1, v.ndim - 1))
    after = jnp.where(lane == CZ - 1, 0.0, pltpu.roll(v, CZ - 1, v.ndim - 1))
    return before + after


def pick(table, classes):
    low, mid, high = (classes & 1) == 1, (classes & 2) == 2, (classes & 4) == 4
    pairs = [jnp.where(low, table[2 * i + 1], table[2 * i]) for i in range(4)]
    return jnp.where(high, jnp.where(mid, pairs[3], pairs[2]), jnp.where(mid, pairs[1], pairs[0]))


def open_sides():
    sides = []
    for axis in ("span", "pitch", "chord"):
        position, size = lax.axis_index(axis), lax.axis_size(axis)
        sides.append(jnp.where(position > 0, 1.0, 0.0).astype(jnp.float32))
        sides.append(jnp.where(position < size - 1, 1.0, 0.0).astype(jnp.float32))
    return sides


def slots(shape):
    lane = iota(shape, len(shape) - 1)
    plane = (lane * 43) >> 8
    return plane, lane - 6 * plane


def column_kernel(
    table_in, start, source, classes, p0, cs, stiffness, z_low, z_high,
    table, y_in, s_in, c_in, beyond, sems, table_sem,
):
    table_copy = pltpu.make_async_copy(table_in, table, table_sem)
    table_copy.start()
    copies = []
    for g in range(CX // STEP_X):
        part = pl.ds(g * STEP_X, STEP_X)
        copies.append(
            [
                pltpu.make_async_copy(classes.at[part], c_in.at[part], sems.at[0, g]),
                pltpu.make_async_copy(start.at[:, part], y_in.at[:, part], sems.at[1, g]),
                pltpu.make_async_copy(source.at[:, part], s_in.at[:, part], sems.at[2, g]),
            ]
        )
        for copy in copies[-1]:
            copy.start()
    x_lo, x_hi, y_lo, y_hi, z_lo, z_hi = open_sides()

    lane = iota((CY, CZ), 1)
    edge = (lane < 3) | (lane >= CZ - 3)
    values = [jnp.zeros((CY, CZ), jnp.float32) for _ in range(3)]
    pushes = [jnp.zeros((CY, CZ), jnp.float32) for _ in range(3)]
    table_copy.wait()
    for x in range(CX):
        if x % STEP_X == 0:
            for copy in copies[x // STEP_X]:
                copy.wait()
        k = pick(table, c_in[x])
        stiffness[x] = k
        shift = (6 * (x + 2) + 3) % CZ
        for c in range(3):
            value = k * y_in[c, x]
            push = STEP * s_in[c, x]
            p0[c, x] = value
            cs[c, x] = push
            values[c] = values[c] + pltpu.roll(jnp.where(edge, value, 0.0), shift, 1)
            pushes[c] = pushes[c] + pltpu.roll(jnp.where(edge, push, 0.0), shift, 1)

    shape = (GY, CZ)
    plane, slot = slots(shape)
    row = iota(shape, 0)
    keep = jnp.where(row < 8, y_lo, jnp.where(row >= 8 + CY, y_hi, 1.0))
    side = jnp.where(plane < 2, x_lo, jnp.where(plane >= 2 + CX, x_hi, 1.0))
    side = jnp.where(plane < 20, side, 0.0) * keep
    at_high, at_low = slot == 2, slot == 3
    gate = jnp.where(at_high, z_hi, jnp.where(at_low, z_lo, 0.0))
    no_before, no_after = (slot == 0) | (slot == 3), (slot == 2) | (slot == 5)
    pad = jnp.zeros((8, CZ), jnp.float32)
    _, packed_slot = slots((HALF, CZ))

    for c in range(3):
        along = PULL[c][2]

        def flat(v):
            planes = pltpu.roll(v, 6, 1) + pltpu.roll(v, CZ - 6, 1)
            lines = pltpu.roll(v, 1, 0) + pltpu.roll(v, GY - 1, 0)
            return (OWN * v + PULL[c][0] * planes + PULL[c][1] * lines) * side

        def beside(v):
            before = jnp.where(no_before, 0.0, pltpu.roll(v, 1, 1))
            after = jnp.where(no_after, 0.0, pltpu.roll(v, CZ - 1, 1))
            return along * (before + after)

        v0 = jnp.concatenate([pad, values[c], pad], axis=0)
        push = jnp.concatenate([pad, pushes[c], pad], axis=0)
        t1 = flat(v0)
        v1 = t1 + beside(v0) + push
        t2 = flat(v1)
        v2 = t2 + beside(v1) + push + (along * along) * gate * v0
        out1 = along * gate * (flat(t1) + t2 + v2 + (along * along) * v0)
        out2 = (along * along) * gate * (2.0 * t1 + v1)
        out3 = (along * along * along) * gate * v0
        given = jnp.zeros(shape, jnp.float32)
        for far, out in ((1, out1), (2, out2), (3, out3)):
            given = given + pltpu.roll(jnp.where(at_low, out, 0.0), CZ - far, 1)
            given = given + pltpu.roll(jnp.where(at_high, out, 0.0), far, 1)
        beyond[c] = given
        top, rest = beyond[c, FIRST:MIDDLE, :], beyond[c, MIDDLE:LAST, :]
        rows = slice(HALF * c, HALF * (c + 1))
        z_low[rows, :] = jnp.where(packed_slot < 3, top, pltpu.roll(rest, 3, 1))
        z_high[rows, :] = jnp.where(packed_slot >= 3, rest, pltpu.roll(top, CZ - 3, 1))
    for out in (z_low, z_high):
        out[3 * HALF : 56, :] = jnp.zeros((56 - 3 * HALF, CZ), jnp.float32)


def sweep_kernel(p0_in, cs_in, inner, y_low, y_high, x_out, p0, p1, p2, q, cs):
    x_lo, x_hi, y_lo, y_hi, z_lo, z_hi = open_sides()
    shape = (GY, CZ)
    row, lane = iota(shape, 0), iota(shape, 1)
    keep = jnp.where(row < 8, y_lo, jnp.where(row >= 8 + CY, y_hi, 1.0))
    gate = jnp.where(lane == 0, z_lo, jnp.where(lane == CZ - 1, z_hi, 0.0))
    zeros = jnp.zeros(shape, jnp.float32)

    def clear(ref, planes):
        for c in range(3):
            for x in planes:
                ref[c, x] = zeros

    clear(p0, (2, 3, 20, 21))
    clear(p1, (1, 2, 21, 22))
    clear(p2, (0, 1, 22, 23))
    clear(q, (1, 2, 21, 22))
    clear(cs, (1, 2, 3, 20, 21, 22))
    pad = jnp.zeros((8, CZ), jnp.float32)
    for x in range(CX):
        for c in range(3):
            for ref, given in ((p0, p0_in), (cs, cs_in)):
                ref[c, x + 4, 0:8, :] = pad
                ref[c, x + 4, 8 : 8 + CY, :] = given[c, x]
                ref[c, x + 4, 8 + CY : GY, :] = pad

    def across(ref, c, x):
        here = ref[c, x]
        planes = ref[c, x - 1] + ref[c, x + 1]
        lines = pltpu.roll(here, 1, 0) + pltpu.roll(here, GY - 1, 0)
        side = jnp.where(x < 4, x_lo, jnp.where(x >= 4 + CX, x_hi, 1.0))
        return here, (OWN * here + PULL[c][0] * planes + PULL[c][1] * lines) * (keep * side)

    def first(x, carry):
        for c in range(3):
            here, flat = across(p0, c, x)
            new = flat + PULL[c][2] * shifted_lanes(here) + cs[c, x]
            p1[c, x] = new
            q[c, x] = flat + new
        return carry

    lax.fori_loop(3, 21, first, 0, unroll=True)

    def second(x, carry):
        for c in range(3):
            here, flat = across(p1, c, x)
            new = flat + PULL[c][2] * shifted_lanes(here) + cs[c, x]
            p2[c, x] = new + (PULL[c][2] * PULL[c][2] * gate) * p0[c, x]
        return carry

    lax.fori_loop(2, 22, second, 0, unroll=True)

    def third(x):
        values = []
        for c in range(3):
            here, flat = across(p2, c, x)
            new = flat + PULL[c][2] * shifted_lanes(here) + cs[c, x]
            new = new + (PULL[c][2] * PULL[c][2] * gate) * q[c, x]
            y_low[c, x] = new[0:8, :]
            y_high[c, x] = new[8 + CY : GY, :]
            values.append(new[8 : 8 + CY, :])
        return values

    for i, x in enumerate((1, 2, 3, 20, 21, 22)):
        for c, value in enumerate(third(x)):
            x_out[c, i] = value

    def middle(x, carry):
        for c, value in enumerate(third(x)):
            inner[c, x - 4] = value
        return carry

    lax.fori_loop(4, 20, middle, 0, unroll=True)


def unpack(z_next, z_prev, columns):
    _, slot = slots((HALF, CZ))
    for c in range(3):
        rows = slice(HALF * c, HALF * (c + 1))
        above, below = z_next[rows, :], z_prev[rows, :]
        columns[c, 0:8, :] = jnp.zeros((8, CZ), jnp.float32)
        columns[c, GY - 8 : GY, :] = jnp.zeros((8, CZ), jnp.float32)
        columns[c, FIRST:MIDDLE, :] = jnp.where(slot < 3, above, pltpu.roll(below, 3, 1))
        columns[c, MIDDLE:LAST, :] = jnp.where(slot < 3, pltpu.roll(above, CZ - 3, 1), below)


def chord_part(columns, c, x, start, size):
    lane = iota((size, CZ), 1)
    placed = pltpu.roll(columns[c, start : start + size, :], (CZ - 3 - 6 * (x - 2)) % CZ, 1)
    return jnp.where((lane < 3) | (lane >= CZ - 3), placed, 0.0)


def pitch_kernel(y_low, y_high, z_next, z_prev, low, high, columns):
    unpack(z_next, z_prev, columns)
    for c in range(3):
        for x in range(1, 23):
            for tile, out, start, first in ((y_low, low, 0, 5), (y_high, high, 40, 0)):
                value = tile[c, x]
                if 2 <= x < 22:
                    value = value + chord_part(columns, c, x, start, 8)
                for j in range(3):
                    out[c, j, x : x + 1, :] = value[first + j : first + j + 1, :]


def pitch_rows(y_next, y_prev, c, x):
    row = iota((8, CZ), 0)
    bottom = jnp.zeros((8, CZ), jnp.float32)
    top = jnp.zeros((8, CZ), jnp.float32)
    for j in range(3):
        bottom = jnp.where(row == j, y_prev[c, j, x : x + 1, :], bottom)
        top = jnp.where(row == 5 + j, y_next[c, j, x : x + 1, :], top)
    return bottom, top


def span_kernel(x_out, z_next, z_prev, y_next, y_prev, low, high, columns):
    unpack(z_next, z_prev, columns)
    for c in range(3):
        for i, x in enumerate((1, 2, 3, 20, 21, 22)):
            out, j = (low, i) if i < 3 else (high, i - 3)
            value = x_out[c, i]
            if 2 <= x < 22:
                value = value + chord_part(columns, c, x, 8, CY)
            out[c, j] = value
            bottom, top = pitch_rows(y_next, y_prev, c, x)
            out[c, j, 0:8, :] += bottom
            out[c, j, 24:32, :] += top


def finish_planes(planes, inner, z_next, z_prev, y_next, y_prev, stiffness, columns, values, part, field, span):
    unpack(z_next, z_prev, columns)
    zeros = jnp.zeros((8, CZ), jnp.float32)
    for i, x in enumerate(planes):
        ratio = 1.0 / stiffness[x]
        for c in range(3):
            value = inner[c, x] + chord_part(columns, c, x + 4, 8, CY)
            bottom, top = pitch_rows(y_next, y_prev, c, x + 4)
            value = value + jnp.concatenate([bottom, zeros, zeros, top], axis=0)
            value = span(value, c, x)
            values[c, i] = value * ratio
            part[c, CY * i : CY * (i + 1), :] = value
    for c in range(3):
        for g in range(CY * len(planes) // 128):
            block = part[c, 128 * g : 128 * (g + 1), :].T
            first = block.astype(jnp.bfloat16)
            second = (block - first.astype(jnp.float32)).astype(jnp.bfloat16)
            field[256 * c : 256 * c + 128, 128 * g : 128 * (g + 1)] = first
            field[256 * c + 128 : 256 * c + 256, 128 * g : 128 * (g + 1)] = second


def marks(length, place):
    return (iota((length, place.shape[1]), 0) == place).astype(jnp.bfloat16)


def mark_kernel(wall_cell, patch_owner, after, planes, patches):
    for step in range(WALL // 512):
        here = slice(step * 512, (step + 1) * 512)
        plane = wall_cell[:, here] >> 7
        place = jnp.where(plane < 128, plane, jnp.where(plane >= 384, plane - 256, -1))
        planes[:, here] = marks(256, place)
        patches[here, :] = marks(PATCH_DEV, patch_owner[:, here] & 127).T


def normal_share(field, planes, cell, normals):
    count = cell.shape[1]
    picked = jnp.dot(field[...], planes, preferred_element_type=jnp.float32)
    value = jnp.zeros((CZ, count), jnp.float32)
    for c in range(3):
        part = picked[256 * c : 256 * c + 128] + picked[256 * c + 128 : 256 * c + 256]
        value = value + normals[c : c + 1] * part
    value = jnp.where(iota((CZ, count), 0) == (cell & 127), value, 0.0)
    return jnp.sum(value, axis=0, keepdims=True)


def middle_kernel(
    inner, stiffness, z_next, z_prev, y_next, y_prev, wall_cell, wall_normal,
    adjoint, share, columns, values, part, field, sem,
):
    def as_is(value, c, x):
        return value

    finish_planes(
        range(4, 12), inner, z_next, z_prev, y_next, y_prev,
        stiffness, columns, values, part, field, as_is,
    )
    copy = pltpu.make_async_copy(values, adjoint.at[:, 4:12], sem)
    copy.start()
    for step in range(WALL // ROWS):
        here = slice(step * ROWS, (step + 1) * ROWS)
        cell = wall_cell[:, here]
        share[:, here] = normal_share(
            field, marks(256, (cell >> 7) - 128), cell, wall_normal[:, here]
        )
    copy.wait()


def wall_kernel(
    given, inner, stiffness, z_next, z_prev, y_next, y_prev, x_prev, x_next, share,
    wall_cell, patch_owner, wall_normal, mode_shape, planes, patches,
    adjoint, sums, columns, values, part, field, sems,
):
    def span(value, c, x):
        if x < 3:
            return value + x_prev[c, x]
        if x >= CX - 3:
            return value + x_next[c, x - (CX - 3)]
        return value

    finish_planes(
        (0, 1, 2, 3, 12, 13, 14, 15), inner, z_next, z_prev, y_next, y_prev,
        stiffness, columns, values, part, field, span,
    )
    copies = [
        pltpu.make_async_copy(values.at[:, 0:4], adjoint.at[:, 0:4], sems.at[0]),
        pltpu.make_async_copy(values.at[:, 4:8], adjoint.at[:, 12:16], sems.at[1]),
    ]
    for copy in copies:
        copy.start()
    total = jnp.zeros((2 * CHORD * MODES, PATCH_DEV), jnp.float32)
    for step in range(WALL // ROWS):
        here = slice(step * ROWS, (step + 1) * ROWS)
        cell, owner = wall_cell[:, here], patch_owner[:, here]
        normal = share[:, here] + normal_share(field, planes[:, here], cell, wall_normal[:, here])
        parts = mode_shape[:, here] * normal
        high = parts.astype(jnp.bfloat16).astype(jnp.float32)
        pieces = jnp.concatenate([high, parts - high], axis=0).astype(jnp.bfloat16)
        device = jnp.broadcast_to((owner >> 7).astype(jnp.float32), pieces.shape).astype(jnp.bfloat16)
        both = jnp.concatenate(
            [jnp.where(device == o, pieces, jnp.bfloat16(0)) for o in range(CHORD)], axis=0
        )
        total = total + jnp.dot(both, patches[here, :], preferred_element_type=jnp.float32)
    for o in range(CHORD):
        first, second = 2 * MODES * o, MODES * (2 * o + 1)
        sums[MODES * o : MODES * (o + 1), :] = total[first : first + MODES] + total[second : second + MODES]
    for copy in copies:
        copy.wait()


def call(
    kernel, outs, operands, spaces, scratch=(), out_spaces=None, aliases=None, flops=0, kind=jnp.float32
):
    spec = {"h": HBM, "s": SMEM, "v": VMEM}
    shapes = tuple(jax.ShapeDtypeStruct(shape, kind) for shape in outs)
    moved = sum(4 * o.size for o in operands) + sum(4 * s.size for s in shapes)
    operands = [
        pltpu.with_memory_space_constraint(o, pltpu.HBM) if space == "h" else o
        for o, space in zip(operands, spaces)
    ]
    return pl.pallas_call(
        kernel,
        out_shape=shapes,
        in_specs=[spec[space] for space in spaces],
        out_specs=tuple(spec[space] for space in out_spaces or "v" * len(outs)),
        scratch_shapes=list(scratch),
        input_output_aliases=aliases or {},
        cost_estimate=pl.CostEstimate(flops=flops, bytes_accessed=moved, transcendentals=0),
        compiler_params=pltpu.CompilerParams(vmem_limit_bytes=40 << 20),
    )(*operands)


def pairs(axis):
    return [(i, i + 1) for i in range(lax.axis_size(axis) - 1)]


def from_next(low, axis):
    return lax.ppermute(low, axis, [(j, i) for i, j in pairs(axis)])


def from_previous(high, axis):
    return lax.ppermute(high, axis, pairs(axis))


def body(
    adjoint_start,
    sensitivity_source,
    stiffness_class,
    stiffness_table,
    wall_cell,
    patch_owner,
    wall_normal,
    mode_shape,
):
    block, columns = (3, CX, CY, CZ), pltpu.VMEM((3, GY, CZ), jnp.float32)
    grown = pltpu.VMEM((3, GX, GY, CZ), jnp.float32)
    p0, cs, stiffness, z_low, z_high = call(
        column_kernel,
        (block, block, (CX, CY, CZ), (56, CZ), (56, CZ)),
        (stiffness_table, adjoint_start, sensitivity_source, stiffness_class),
        "hhhh",
        scratch=(
            pltpu.SMEM((8,), jnp.float32),
            pltpu.VMEM(block, jnp.float32),
            pltpu.VMEM(block, jnp.float32),
            pltpu.VMEM((CX, CY, CZ), jnp.int32),
            columns,
            pltpu.SemaphoreType.DMA((3, CX // STEP_X)),
            pltpu.SemaphoreType.DMA,
        ),
    )
    z_prev, z_next = from_previous(z_high, "chord"), from_next(z_low, "chord")
    inner, y_low, y_high, x_out = call(
        sweep_kernel,
        (block, (3, GX, 8, CZ), (3, GX, 8, CZ), (3, 6, CY, CZ)),
        (p0, cs),
        "vv",
        scratch=(grown,) * 5,
        flops=1 << 25,
    )
    cells, owners = wall_cell.reshape(1, WALL), patch_owner.reshape(1, WALL)
    planes, patches = call(
        mark_kernel,
        ((256, WALL), (WALL, PATCH_DEV)),
        (cells, owners, y_low),
        "vvv",
        flops=1 << 25,
        kind=jnp.bfloat16,
    )
    y_low, planes, patches = lax.optimization_barrier((y_low, planes, patches))
    slab = (3, 3, GX, CZ)
    low, high = call(
        pitch_kernel, (slab, slab), (y_low, y_high, z_next, z_prev), "vvvv", scratch=(columns,)
    )
    y_next, y_prev = from_next(low, "pitch"), from_previous(high, "pitch")
    slab = (3, 3, CY, CZ)
    low, high = call(
        span_kernel, (slab, slab), (x_out, z_next, z_prev, y_next, y_prev), "vvvvv", scratch=(columns,)
    )
    x_prev, x_next = from_previous(high, "span"), from_next(low, "span")
    given = (z_next, z_prev, y_next, y_prev)
    work = (
        columns,
        pltpu.VMEM((3, CX // 2, CY, CZ), jnp.float32),
        pltpu.VMEM((3, CX // 2 * CY, CZ), jnp.float32),
        pltpu.VMEM((6 * CZ, CX // 2 * CY), jnp.bfloat16),
    )
    adjoint, share = call(
        middle_kernel,
        (block, (1, WALL)),
        (inner, stiffness, *given, cells, wall_normal),
        "vvvvvvvv",
        scratch=(*work, pltpu.SemaphoreType.DMA),
        out_spaces="hv",
        flops=1 << 30,
    )
    adjoint, sums = call(
        wall_kernel,
        (block, (CHORD * MODES, PATCH_DEV)),
        (
            adjoint, inner, stiffness, *given, x_prev, x_next, share,
            cells, owners, wall_normal, mode_shape, planes, patches,
        ),
        "hvvvvvvvvvvvvvvv",
        scratch=(*work, pltpu.SemaphoreType.DMA((2,))),
        out_spaces="hv",
        aliases={0: 0},
        flops=1 << 30,
    )
    sums = sums.reshape(CHORD, MODES, PATCH_DEV)
    arrived = lax.all_to_all(sums, "chord", split_axis=0, concat_axis=0, tiled=True)
    return adjoint, arrived.sum(axis=0)


def solution(mesh):
    in_specs = (
        P(None, "span", "pitch", "chord"),
        P(None, "span", "pitch", "chord"),
        P("span", "pitch", "chord"),
        P(),
        P(("span", "pitch", "chord")),
        P(("span", "pitch", "chord"), None),
        P(None, ("span", "pitch", "chord")),
        P(None, ("span", "pitch", "chord")),
    )
    out_specs = (P(None, "span", "pitch", "chord"), P(None, ("span", "pitch", "chord")))
    return jax.shard_map(body, mesh=mesh, in_specs=in_specs, out_specs=out_specs, check_vma=False)
```
